32 devices in a mesh: groups: 2 (over x), patch: 8 (over z, y), section: 2 (over core).
Axes of the slice: x: 2, y: 2, z: 4, core: 2. Of those that a mesh axis runs over, the one named last changes fastest.
Arguments:
- hidden_in: bfloat16 [6144, 3072], P(('groups', 'patch')), parts along dimension 0, may hold values from -6 to 6
- text_rows: bfloat16 [256, 3072], P('groups', 'patch'), parts along dimension 0, may hold values from -6 to 6
- mod_table: float32 [50, 2, 5, 3072], P(None, 'section'), may hold values from -3 to 3
- timestep: int32 [2], P('groups'), parts along dimension 0, may hold values from 0 to 49
- w_query: bfloat16 [2, 3072, 1536], P('section', 'patch'), may hold values from -0.109375 to 0.109375
- w_out: bfloat16 [2, 1536, 3072], P('section', 'patch'), may hold values from -1.25 to 1.25
- w_text: bfloat16 [2, 3072, 3072], P('section', 'patch'), may hold values from -0.109375 to 0.109375
- stale_kv: bfloat16 [2, 6144, 3072], P('section', ('groups', 'patch')), parts along dimension 1, may hold values from -450 to 450
- mask_blocks: int32 [48, 4], P(('groups', 'patch')), parts along dimension 0, may hold values from 0 to 23, as said below
- counts: int32 [48], P(('groups', 'patch')), parts along dimension 0, may hold values from 1 to 4, as said below
Outputs:
- hidden_out: bfloat16 [2, 6144, 3072], P('section', ('groups', 'patch')), parts along dimension 1
The draws below stay inside these ranges and needn't reach their ends.
There are 2 independent parts, one for each index of `groups`. The reference program is written for one: setup_inputs(seed, part) draws one part's arguments, and reference() takes and returns one part's arrays. A program takes and returns all parts, laid end to end along the dimension named above; an argument that names none is the same for every part. Nothing has to cross between parts.
Inputs may be any that keep to these rules, and one draw needn't show every extreme that they name: `mask_blocks`: row b lists 4 different block numbers, b itself first; every one is a block stored on the same patch device as block b or on the device just before or after it (384 tokens a device, blocks of 128 tokens). Only the first counts[b] entries of row b of mask_blocks are used; some block has 4.
All inputs are finite; a program needn't handle non-finite values.
Results may differ from the reference program's by a relative error of at most 0.037.
Values may be sent and summed in bfloat16 or wider, within the bound.
A program may use at most 128 MiB of HBM per device.

```python
import jax
import jax.numpy as jnp
from jax import lax

D = 3072
HEADS = 12
HD = 128
INNER = 1536
BLK = 128
WIN = 4
TXT = 128
STEPS = 50
TOK_DEV = 384
SEQ = 3072
NBLK = 24
LAYERS = 2


def draw_mask_blocks(key, part):
    per_device = TOK_DEV // BLK
    span = 3 * per_device
    block = jnp.arange(NBLK, dtype=jnp.int32)
    home = block // per_device
    offsets = jnp.arange(span, dtype=jnp.int32)
    candidate = (home[:, None] - 1) * per_device + offsets[None, :]
    usable = (candidate >= 0) & (candidate < NBLK) & (candidate != block[:, None])
    noise = jax.random.randint(jax.random.fold_in(key, 7), (NBLK, span), 0, 1 << 18)
    score = jnp.where(usable, noise * span + offsets[None, :], (1 << 30) + offsets[None, :])
    order = jnp.argsort(score, axis=1, stable=True)
    picked = jnp.take_along_axis(candidate, order[:, :WIN - 1], axis=1)
    return jnp.concatenate([block[:, None], picked], axis=1).astype(jnp.int32)


def draw_counts(key, part):
    base = jax.random.randint(jax.random.fold_in(key, 13), (NBLK,), 1, WIN + 1)
    filled = jax.random.randint(jax.random.fold_in(key, 17), (), 0, NBLK)
    return jnp.where(jnp.arange(NBLK) == filled, WIN, base).astype(jnp.int32)


def draw_stale_kv(key, part):
    shape = (LAYERS, SEQ, 2 * INNER)
    base = jax.random.normal(jax.random.fold_in(key, 3), shape, jnp.float32)
    return jnp.clip(base, -6.0, 6.0).astype(jnp.bfloat16)


def levels(own_key, dims, split, least, top_value):
    factor_of, own = 1.0, jax.random.fold_in(own_key, 6)
    for dim, parts in split:
        draws = jnp.exp(jax.random.uniform(jax.random.fold_in(own, dim), (parts,), jnp.float32, least / len(split), top_value / len(split)))
        factor_of = factor_of * jnp.repeat(draws, dims[dim] // parts).reshape([-1 if axis == dim else 1 for axis in range(len(dims))])
    return factor_of


def scatter_about(rng, dims, deviation, bound, cuts=(), kind=jnp.bfloat16):
    loudness = levels(rng, dims, cuts, -0.22, 0.18) if cuts else 1.0
    drawn = jax.random.normal(rng, dims, jnp.float32) * deviation * loudness
    return jnp.minimum(jnp.maximum(drawn, -bound), bound).astype(kind)


def setup_inputs(seed: int = 0, part: int = 0) -> dict:
    splits = jax.random.split(jax.random.key(seed), 11)
    part_keys = jax.random.split(jax.random.fold_in(splits[10], part), 11)
    hidden_in = scatter_about(part_keys[0], (SEQ, D), 1.0, 6.0, ((0, 8),))
    text_rows = scatter_about(part_keys[1], (TXT, D), 1.0, 6.0, ((1, 8),))
    mod_table = scatter_about(splits[2], (STEPS, LAYERS, 5, D), 0.5, 3.0, ((1, 2),), jnp.float32)
    timestep = jax.random.randint(part_keys[3], (1,), 0, STEPS).astype(jnp.int32)
    w_query = scatter_about(splits[4], (LAYERS, D, INNER), D ** -0.5, 0.109375, ((0, 2), (1, 8)))
    w_out = scatter_about(splits[5], (LAYERS, INNER, D), (max(INNER // 64, 1)) ** -0.5, 1.25, ((0, 2), (1, 8)))
    w_text = scatter_about(splits[6], (LAYERS, D, 2 * INNER), D ** -0.5, 0.109375, ((0, 2), (1, 8)))
    stale_kv = draw_stale_kv(jax.random.fold_in(jax.random.fold_in(splits[10], part), 71), part)
    mask_blocks = draw_mask_blocks(jax.random.fold_in(jax.random.fold_in(splits[10], part), 71), part)
    counts = draw_counts(jax.random.fold_in(jax.random.fold_in(splits[10], part), 71), part)
    return dict(hidden_in=hidden_in, text_rows=text_rows, mod_table=mod_table, timestep=timestep, w_query=w_query, w_out=w_out, w_text=w_text, stale_kv=stale_kv, mask_blocks=mask_blocks, counts=counts)


EPSILON = 1e-06

def layer_norm(values):
    values = values.astype(jnp.float32)
    center = values - lax.optimization_barrier(jnp.mean(values, axis=-1, keepdims=True))
    spread = lax.optimization_barrier(jnp.mean(center * center, axis=-1, keepdims=True))
    return center * lax.rsqrt(spread + EPSILON)

def attend(block_query, image_pairs, text_pairs, live_count):
    joined = jnp.concatenate([text_pairs, image_pairs], axis=0)
    slot = jnp.arange(WIN * BLK, dtype=jnp.int32) // BLK
    live = jnp.concatenate([jnp.ones((TXT,), dtype=jnp.bool_), slot < live_count])
    keys = joined[:, :INNER].astype(jnp.float32).reshape(-1, HEADS, HD)
    values = joined[:, INNER:].astype(jnp.float32).reshape(-1, HEADS, HD)
    query_heads = block_query.astype(jnp.float32).reshape(BLK, HEADS, HD)
    scores = jnp.einsum('qhd,khd->hqk', query_heads, keys) * HD ** (-0.5)
    scores = jnp.where(live[None, None, :], scores, -1e+30)
    peak = lax.optimization_barrier(jnp.max(scores, axis=-1, keepdims=True))
    raised = jnp.exp(scores - peak)
    probs = (raised / lax.optimization_barrier(jnp.sum(raised, axis=-1, keepdims=True))).astype(jnp.bfloat16)
    mixed = jnp.einsum('hqk,khd->qhd', probs.astype(jnp.float32), values)
    return mixed.reshape(BLK, INNER).astype(jnp.bfloat16)

def reference(hidden_in, text_rows, mod_table, timestep, w_query, w_out, w_text, stale_kv, mask_blocks, counts):
    modulations = lax.dynamic_index_in_dim(mod_table, timestep[0], 0, keepdims=False)
    state = hidden_in
    results = []
    for layer in range(LAYERS):
        modulation = modulations[layer]
        conditioned = (text_rows.astype(jnp.float32) * (1.0 + modulation[4]) + modulation[3]).astype(jnp.bfloat16)
        text_pairs = jnp.dot(conditioned, w_text[layer], preferred_element_type=jnp.float32).astype(jnp.bfloat16)
        normed = (layer_norm(state) * (1.0 + modulation[1]) + modulation[0]).astype(jnp.bfloat16)
        query = jnp.dot(normed, w_query[layer], preferred_element_type=jnp.float32).astype(jnp.bfloat16)
        stale_blocks = stale_kv[layer].reshape(NBLK, BLK, 2 * INNER)

        def per_block(items):
            block_query, chosen, live_count = items
            image_pairs = jnp.take(stale_blocks, chosen, axis=0).reshape(WIN * BLK, 2 * INNER)
            return attend(block_query, image_pairs, text_pairs, live_count)
        attended = lax.map(per_block, (query.reshape(NBLK, BLK, INNER), mask_blocks, counts))
        attended = attended.reshape(SEQ, INNER)
        projected = jnp.dot(attended, w_out[layer], preferred_element_type=jnp.float32)
        state = (state.astype(jnp.float32) + modulation[2] * projected).astype(jnp.bfloat16)
        results.append(state)
    return jnp.stack(results, axis=0)
```

```python
import functools

import jax
import jax.numpy as jnp
from jax import lax
from jax.experimental import pallas as pl
from jax.experimental.pallas import tpu as pltpu
from jax.sharding import PartitionSpec as P

HD = 128
BLK = 128
EPSILON = 1e-06
MESH = pl.DeviceIdType.MESH
ROWS = 16


def exclusive_rows(rows):
    return max(rows * 5 // 12 // ROWS, 1) * ROWS


TILE = 256


def kernel(
    n, chosen, counts, modulation, state, wq, wo, kv, part, out,
    wq_all, wo_all, kvs, text, sums, total, normed, query, mixed, inbox,
    ring_send, ring_recv, mate_send, mate_recv, rim_send, rim_recv,
    text_send, text_recv, share_send, share_recv, hand_send, hand_recv, own_sem, text_sem, gate,
):
    me = lax.axis_index("patch")
    group = lax.axis_index("groups")
    section = lax.axis_index("section")
    parity = lax.rem(group, 2)
    mate = group + 1 - 2 * parity
    half = n // 2
    odd = lax.rem(me, 2)
    place = (1 - odd) * lax.div(me, 2) + odd * (n - 1 - lax.div(me, 2))
    tokens, width = state.shape
    inner = query.shape[1]
    heads = inner // HD
    blocks = kv.shape[0]
    chunks = part.shape[0]
    spread = chosen.shape[1]
    lead = text.shape[0]
    keys = lead + spread * BLK

    def at(position):
        position = lax.rem(position + n, n)
        high = lax.div(position, half)
        return (1 - high) * 2 * position + high * (2 * (n - 1 - position) + 1)

    def when(condition, action):
        if isinstance(condition, bool):
            if condition:
                action()
        else:
            pl.when(condition)(action)

    right, left = at(place + 1), at(place - 1)

    own_copies = [
        pltpu.make_async_copy(wq, wq_all.at[pl.ds(pl.multiple_of(me * wq.shape[0], ROWS), wq.shape[0])], own_sem.at[0]),
        pltpu.make_async_copy(wo, wo_all.at[pl.ds(pl.multiple_of(me * wo.shape[0], ROWS), wo.shape[0])], own_sem.at[1]),
        pltpu.make_async_copy(kv, kvs.at[pl.ds(blocks, blocks)], own_sem.at[2]),
    ]

    barrier = pltpu.get_barrier_semaphore()
    for step in range(1, n):
        pl.semaphore_signal(barrier, inc=1, device_id={"patch": lax.rem(me + step, n)}, device_id_type=MESH)
    pl.semaphore_signal(barrier, inc=1, device_id={"groups": mate}, device_id_type=MESH)
    pl.semaphore_signal(barrier, inc=1, device_id={"section": 1 - section}, device_id_type=MESH)
    pl.semaphore_wait(barrier, n + 1)

    matrices = ((wq, wq_all), (wo, wo_all))
    ways = (-1, 1)

    def reach(side, way):
        return half - (side + way) % 2

    def remote(src, dst, send, recv, target):
        return pltpu.make_async_remote_copy(
            src_ref=src, dst_ref=dst, send_sem=send, recv_sem=recv,
            device_id=target, device_id_type=MESH,
        )

    def span(start, size, unit=ROWS):
        return pl.ds(start if isinstance(start, int) else pl.multiple_of(start, unit), size)

    def ring(matrix, side, way, hop, received=False, first=False):
        own, every = matrices[matrix]
        rows, cut = own.shape[0], own.shape[1] // 2
        apart = exclusive_rows(rows)
        keep = rows - apart
        columns = span(side * cut, cut, HD)
        shard = at(place + ways[way] * (hop if received else hop - 1))
        dst = every.at[span(shard * rows + parity * apart, keep), columns]
        src = own.at[span(parity * apart, keep), columns] if first else dst
        target = {"patch": left if way else right}
        flow = matrix * 4 + side * 2 + way
        return remote(src, dst, ring_send.at[flow, hop - 1], ring_recv.at[flow, hop - 1], target)

    def across(matrix, side, way, hop, received=False):
        own, every = matrices[matrix]
        rows, cut = own.shape[0], own.shape[1] // 2
        apart = exclusive_rows(rows)
        keep = rows - apart
        shard = at(place + ways[way] * hop)
        whose = 1 - parity if received else parity
        ref = every.at[span(shard * rows + whose * keep, apart), span(side * cut, cut, HD)]
        flow = matrix * 4 + side * 2 + way
        return remote(ref, ref, mate_send.at[flow, hop - 1], mate_recv.at[flow, hop - 1], {"groups": mate})

    def launch(matrix):
        for side in range(2):
            for way in range(2):
                ring(matrix, side, way, 1, first=True).start()

    def relay(matrix, step):
        hop, side = step // 2 + 1, step % 2
        for way in range(2):
            far = reach(side, way)

            def pass_on():
                ring(matrix, side, way, hop, received=True).wait_recv()
                when(hop < far, lambda: ring(matrix, side, way, hop + 1).start())
                across(matrix, side, way, hop).start()

            when(hop <= far, pass_on)

    def gathered(matrix):
        for side in range(2):
            for way in range(2):
                for hop in range(1, reach(side, way) + 1):
                    across(matrix, side, way, hop, True).wait_recv()
        own_copies[matrix].wait()

    pair = me + 1 - 2 * odd
    onward, behind = me + 2 - 4 * odd, me - 2 + 4 * odd
    has_onward = (onward >= 0) & (onward < n)
    has_behind = (behind >= 0) & (behind < n)

    def rim(leg, block, received=False):
        near, far = 2 * (1 - odd) * blocks + block, 2 * odd * blocks + block
        if received:
            dst = kvs.at[far if leg else near]
        else:
            dst = kvs.at[far]
        src = kvs.at[near] if leg else kv.at[block]
        return remote(
            src, dst, rim_send.at[leg, block], rim_recv.at[leg, block],
            {"patch": onward if leg else pair},
        )

    def rim_start():
        for block in range(blocks):
            rim(0, block).start()

    def rim_forward(block):
        rim(0, block, True).wait_recv()
        pl.when(has_onward)(lambda: rim(1, block).start())

    few = chunks < n

    def scatter(step, received=False):
        peer = lax.rem(me + step, n)
        source = lax.rem(me + n - step, n)
        return remote(
            part.at[jnp.minimum(peer, chunks - 1) if few else peer], sums.at[source if received else me],
            text_send.at[step - 1], text_recv.at[step - 1], {"patch": peer},
        )

    def share(step, received=False):
        peer = lax.rem(me + step, n)
        slot = lax.rem(me + n - step, n) if received else me
        ref = text.at[span((jnp.minimum(slot, chunks - 1) if few else slot) * ROWS, ROWS)]
        return remote(ref, ref, share_send.at[step - 1], share_recv.at[step - 1], {"patch": peer})

    own_chunk = jnp.minimum(me, chunks - 1) if few else me
    own_sum = pltpu.make_async_copy(part.at[own_chunk], sums.at[me], text_sem.at[0])
    keep_sum = pltpu.make_async_copy(total, text.at[span(own_chunk * ROWS, ROWS)], text_sem.at[1])

    def held(device):
        return device < chunks if few else True

    def text_start():
        when(held(me), own_sum.start)
        for step in range(1, n):
            when(held(lax.rem(me + step, n)), scatter(step).start)

    def text_reduce():
        def reduce():
            own_sum.wait()
            for step in range(1, n):
                scatter(step, True).wait_recv()
            total[...] = jnp.sum(sums[...].astype(jnp.float32), axis=0).astype(total.dtype)
            keep_sum.start()
            keep_sum.wait()
            for step in range(1, n):
                share(step).start()

        when(held(me), reduce)

    def text_arrive():
        for step in range(1, n):
            when(held(lax.rem(me + n - step, n)), share(step, True).wait_recv)

    def norm(source, first, last):
        @pl.loop(first, last)
        def _(index):
            window = pl.ds(pl.multiple_of(index * ROWS, ROWS), ROWS)
            values = source[window, :].astype(jnp.float32)
            center = values - jnp.mean(values, axis=-1, keepdims=True)
            variance = jnp.mean(center * center, axis=-1, keepdims=True)
            scaled = center * lax.rsqrt(variance + EPSILON)
            normed[window, :] = (
                scaled * (1.0 + modulation[1:2, :]) + modulation[0:1, :]
            ).astype(normed.dtype)

    def project_query(after):
        @pl.loop(0, inner // TILE)
        def _(index):
            window = pl.ds(pl.multiple_of(index * TILE, TILE), TILE)
            query[:, window] = jnp.dot(
                normed[...], wq_all[:, window], preferred_element_type=jnp.float32
            ).astype(query.dtype)
            after(index)

    together = 4 if heads % 4 == 0 else 1
    bunches = heads // together

    def attend(after):
        @pl.loop(0, blocks * bunches)
        def _(index):
            block = lax.div(index, bunches)
            bunch = lax.rem(index, bunches)
            rows = pl.ds(pl.multiple_of(block * BLK, BLK), BLK)
            limit = lead + counts[block] * BLK
            live = lax.broadcasted_iota(jnp.int32, (BLK, keys), 1) < limit
            picks = [
                jnp.clip(chosen[block, slot] - (me - 1) * blocks, 0, 3 * blocks - 1)
                for slot in range(spread)
            ]
            for one in range(together):
                start = bunch * (together * HD) + one * HD
                columns = pl.ds(pl.multiple_of(start, HD), HD)
                beyond = pl.ds(pl.multiple_of(inner + start, HD), HD)
                key = jnp.concatenate([text[:, columns]] + [kvs[pick, :, columns] for pick in picks], axis=0)
                value = jnp.concatenate([text[:, beyond]] + [kvs[pick, :, beyond] for pick in picks], axis=0)
                scores = lax.dot_general(
                    query[rows, columns], key, (((1,), (1,)), ((), ())),
                    preferred_element_type=jnp.float32,
                )
                scores = jnp.where(live, scores, -1e30)
                peak = jnp.max(scores, axis=-1, keepdims=True)
                raised = jnp.exp((scores - peak) * HD ** (-0.5))
                whole = jnp.sum(raised, axis=-1, keepdims=True)
                share_of = jnp.dot(
                    raised.astype(jnp.bfloat16), value, preferred_element_type=jnp.float32
                )
                mixed[rows, columns] = (share_of / whole).astype(mixed.dtype)
            after(index)

    parts = width // (3 * TILE) if width % (3 * TILE) == 0 else 1
    part_width = width // parts

    def project_out(source, index_from, index_to):
        @pl.loop(index_from, index_to)
        def _(index):
            window = pl.ds(pl.multiple_of(index * TILE, TILE), TILE)
            projected = jnp.dot(mixed[...], wo_all[:, window], preferred_element_type=jnp.float32)
            out[:, window] = (
                source[:, window].astype(jnp.float32) + modulation[2:3, window] * projected
            ).astype(out.dtype)

    def hand(index):
        window = pl.ds(index * part_width, part_width)
        return remote(
            out.at[:, window], inbox.at[:, window],
            hand_send.at[index], hand_recv.at[index], {"section": 1 - section},
        )

    def wait_keys():
        own_copies[2].wait()
        for block in range(blocks):
            pl.when(has_behind)(lambda: rim(1, block, True).wait_recv())
        text_arrive()

    steps = 2 * half
    tiles = tokens // ROWS

    def open_gate(index):
        pl.semaphore_signal(gate.at[index], inc=1, device_id={"section": 1 - section}, device_id_type=MESH)

    each = part_width // TILE
    calls = inner // TILE

    def relay_from(base):
        def after(index):
            step = base + index
            pl.when(step < steps)(lambda: relay(1, step))
        return after

    @pl.when(section == 0)
    def _():
        launch(0)
        text_start()
        rim_start()
        for copy in own_copies:
            copy.start()
        forwarded = 0
        for step in range(steps):
            norm(state, step * tiles // steps, (step + 1) * tiles // steps)
            relay(0, step)
            if step == steps // 2:
                text_reduce()
            if step >= 2 and forwarded < blocks:
                rim_forward(forwarded)
                forwarded += 1
            if step == steps - 3:
                launch(1)
        for block in range(forwarded, blocks):
            rim_forward(block)
        open_gate(0)
        gathered(0)
        project_query(lambda index: pl.when(index % 3 == 2)(lambda: relay(1, index // 3)))
        wait_keys()
        attend(lambda index: pl.when((index % 2 == 1) & (index // 2 + 2 < min(4, steps)))(lambda: relay(1, index // 2 + 2)))
        done = min(4, steps)
        for step in range(done, steps):
            if step == steps - 3:
                open_gate(1)
            relay(1, step)
        if steps - 3 < done:
            open_gate(1)
        gathered(1)
        for index in range(parts):
            project_out(state, index * each, (index + 1) * each)
            hand(index).start()

    @pl.when(section == 1)
    def _():
        for copy in own_copies:
            copy.start()
        pl.semaphore_wait(gate.at[0], 1)
        rim_start()
        text_start()
        pl.semaphore_wait(gate.at[1], 1)
        launch(0)
        text_reduce()
        forwarded = 0
        for step in range(steps):
            relay(0, step)
            if forwarded < blocks:
                rim_forward(forwarded)
                forwarded += 1
            if step == steps - 3:
                launch(1)
        for block in range(forwarded, blocks):
            rim_forward(block)
        for index in range(parts):
            hand(index).wait_recv()
        norm(inbox, 0, tiles)
        gathered(0)
        project_query(lambda index: pl.when(index % 3 == 2)(lambda: relay(1, index // 3)))
        wait_keys()
        attend(lambda index: pl.when((index % 2 == 1) & (index // 2 + 2 < min(6, steps)))(lambda: relay(1, index // 2 + 2)))
        for step in range(min(6, steps), steps):
            relay(1, step)
        gathered(1)
        project_out(inbox, 0, width // TILE)

    for matrix in range(2):
        for side in range(2):
            for way in range(2):
                for hop in range(1, reach(side, way) + 1):
                    across(matrix, side, way, hop).wait_send()
                    ring(matrix, side, way, hop).wait_send()
    for step in range(1, n):
        when(held(lax.rem(me + step, n)), scatter(step).wait_send)
        when(held(me), share(step).wait_send)
    for block in range(blocks):
        rim(0, block).wait_send()
        pl.when(has_onward)(lambda: rim(1, block).wait_send())

    @pl.when(section == 0)
    def _():
        for index in range(parts):
            hand(index).wait_send()


def run(n, chosen, counts, modulation, state, wq, wo, kv, part):
    half = n // 2
    tokens, width = state.shape
    inner = wq.shape[1]
    blocks = kv.shape[0]
    smem = pl.BlockSpec(memory_space=pltpu.SMEM)
    vmem = pl.BlockSpec(memory_space=pltpu.VMEM)
    anywhere = pl.BlockSpec(memory_space=pl.ANY)
    dma = pltpu.SemaphoreType.DMA
    parts = width // (3 * TILE) if width % (3 * TILE) == 0 else 1
    b16 = jnp.bfloat16
    return pl.pallas_call(
        functools.partial(kernel, n),
        out_shape=jax.ShapeDtypeStruct(state.shape, state.dtype),
        in_specs=[smem, smem, vmem, vmem] + [anywhere] * 4,
        out_specs=vmem,
        scratch_shapes=[
            pltpu.VMEM((n * wq.shape[0], inner), b16),
            pltpu.VMEM((n * wo.shape[0], width), b16),
            pltpu.VMEM((3 * blocks,) + kv.shape[1:], b16),
            pltpu.VMEM((part.shape[0] * ROWS, kv.shape[2]), b16),
            pltpu.VMEM((n,) + part.shape[1:], part.dtype),
            pltpu.VMEM(part.shape[1:], b16),
            pltpu.VMEM((tokens, width), b16),
            pltpu.VMEM((tokens, inner), b16),
            pltpu.VMEM((tokens, inner), b16),
            pltpu.VMEM((tokens, width), b16),
            dma((8, half)), dma((8, half)), dma((8, half)), dma((8, half)),
            dma((2, blocks)), dma((2, blocks)),
            dma((n - 1,)), dma((n - 1,)), dma((n - 1,)), dma((n - 1,)),
            dma((parts,)), dma((parts,)), dma((3,)), dma((2,)),
            pltpu.SemaphoreType.REGULAR((2,)),
        ],
        compiler_params=pltpu.CompilerParams(
            collective_id=0, has_side_effects=True, vmem_limit_bytes=60 * 2**20
        ),
        name="layers",
    )(chosen, counts, modulation, state, wq, wo, kv, part)


def local(
    hidden_in, text_rows, mod_table, timestep, w_query, w_out, w_text, stale_kv, mask_blocks, counts
):
    patch_id = lax.axis_index("patch")
    n = lax.axis_size("patch")
    width = text_rows.shape[1]
    modulation = lax.dynamic_index_in_dim(mod_table, timestep[0], 0, keepdims=False)[0]
    text_shift = lax.dynamic_slice_in_dim(modulation[3], patch_id * width, width, 0)
    text_scale = lax.dynamic_slice_in_dim(modulation[4], patch_id * width, width, 0)
    conditioned = (text_rows.astype(jnp.float32) * (1.0 + text_scale) + text_shift).astype(
        jnp.bfloat16
    )
    partial_pairs = jnp.dot(conditioned, w_text[0], preferred_element_type=jnp.float32)
    partial_pairs = partial_pairs.astype(jnp.bfloat16)
    kv = stale_kv[0].reshape(-1, BLK, stale_kv.shape[2])
    part = partial_pairs.reshape(-1, ROWS, partial_pairs.shape[1])
    result = run(n, mask_blocks, counts, modulation, hidden_in, w_query[0], w_out[0], kv, part)
    return result[None]


def solution(mesh):
    in_specs = (
        P(("groups", "patch"), None),
        P("groups", "patch"),
        P(None, "section", None, None),
        P("groups"),
        P("section", "patch", None),
        P("section", "patch", None),
        P("section", "patch", None),
        P("section", ("groups", "patch"), None),
        P(("groups", "patch"), None),
        P(("groups", "patch")),
    )
    out_specs = P("section", ("groups", "patch"), None)
    return jax.shard_map(local, mesh=mesh, in_specs=in_specs, out_specs=out_specs, check_vma=False)
```

```python
import functools

import jax
import jax.numpy as jnp
from jax import lax
from jax.experimental import pallas as pl
from jax.experimental.pallas import tpu as pltpu
from jax.sharding import PartitionSpec as P

HD = 128
BLK = 128
EPSILON = 1e-06
MESH = pl.DeviceIdType.MESH
ROWS = 16


def exclusive_rows(rows):
    return max(rows * 5 // 12 // ROWS, 1) * ROWS


TILE = 256


def script_first(steps, blocks):
    sends, onward, text = (-1, 1, 3), (2, 4, 6), (1, 3, 5)
    out = [("launch", 0)] + [("launch", 1)]
    out += [("keys", b) for b in range(blocks) if sends[b] < 0] + [("copies",), ("text",)]
    for s in range(steps):
        out += [("norm", s), ("relay", 0, s)]
        if 0 and s == 2: out += [("launch", 1)]
        if s >= 0: out += [("relay", 1, s - 0)]
        out += [("keys", b) for b in range(blocks) if sends[b] == s]
        if s == text[0]: out += [("fold",)]
        out += [("forward", b) for b in range(blocks) if onward[b] == s]
        if s == text[1]: out += [("reduce",)]
        if s == text[2]: out += [("spread",)]
        if s == 4: out += [("open", 0)]
    rest = list(range(steps - 0, steps))
    out += [("query",) + tuple(zip((2, 5), rest)), ("attend",) + tuple(zip((1, 3), rest[2:]))]
    return out


def script_second(steps, blocks):
    sends, onward, text = (-1, 1, 3), (2, 4, 6), (1, 3, 5)
    out = [("copies",), ("text",), ("pass", 0), ("launch", 0)]
    out += [("keys", b) for b in range(blocks) if sends[b] < 0]
    for s in range(steps):
        out += [("relay", 0, s)]
        if s == 2: out += [("launch", 1)]
        if s >= 4: out += [("relay", 1, s - 4)]
        out += [("keys", b) for b in range(blocks) if sends[b] == s]
        if s == text[0]: out += [("fold",)]
        out += [("forward", b) for b in range(blocks) if onward[b] == s]
        if s == text[1]: out += [("reduce",)]
        if s == text[2]: out += [("spread",)]
    rest = list(range(steps - 4, steps))
    return out, [("query",) + tuple(zip((2, 5), rest)), ("attend",) + tuple(zip((1, 3), rest[2:]))]

def kernel(
    n, chosen, counts, modulation, rows_in, row_mod, state, wq, wo, kv, wt, out,
    wq_all, wo_all, kvs, text, part, fetched, folded, sums, total, normed, query, mixed, inbox,
    ring_send, ring_recv, mate_send, mate_recv, rim_send, rim_recv,
    text_send, text_recv, sums_send, sums_recv, share_send, share_recv, hand_send, hand_recv, own_sem, text_sem, gate,
):
    me = lax.axis_index("patch")
    group = lax.axis_index("groups")
    section = lax.axis_index("section")
    parity = lax.rem(group, 2)
    mate = group + 1 - 2 * parity
    half = n // 2
    odd = lax.rem(me, 2)
    place = (1 - odd) * lax.div(me, 2) + odd * (n - 1 - lax.div(me, 2))
    tokens, width = state.shape
    inner = query.shape[1]
    heads = inner // HD
    blocks = kv.shape[0]
    spread = chosen.shape[1]
    lead = text.shape[0]
    keys = lead + spread * BLK

    def at(position):
        position = lax.rem(position + n, n)
        high = lax.div(position, half)
        return (1 - high) * 2 * position + high * (2 * (n - 1 - position) + 1)

    def when(condition, action):
        if isinstance(condition, bool):
            if condition:
                action()
        else:
            pl.when(condition)(action)

    right, left = at(place + 1), at(place - 1)

    own_copies = [
        pltpu.make_async_copy(wq, wq_all.at[pl.ds(pl.multiple_of(me * wq.shape[0], ROWS), wq.shape[0])], own_sem.at[0]),
        pltpu.make_async_copy(wo, wo_all.at[pl.ds(pl.multiple_of(me * wo.shape[0], ROWS), wo.shape[0])], own_sem.at[1]),
        pltpu.make_async_copy(kv, kvs.at[pl.ds(blocks, blocks)], own_sem.at[2]),
    ]
    fetch_text = pltpu.make_async_copy(wt, out.at[pl.ds(0, wt.shape[0])], own_sem.at[3])
    fetch_state = pltpu.make_async_copy(state, inbox, own_sem.at[4])

    barrier = pltpu.get_barrier_semaphore()
    for step in range(1, n):
        pl.semaphore_signal(barrier, inc=1, device_id={"patch": lax.rem(me + step, n)}, device_id_type=MESH)
    pl.semaphore_signal(barrier, inc=1, device_id={"groups": mate}, device_id_type=MESH)
    pl.semaphore_signal(barrier, inc=1, device_id={"section": 1 - section}, device_id_type=MESH)
    pl.semaphore_wait(barrier, n + 1)

    matrices = ((wq, wq_all), (wo, wo_all))
    ways = (-1, 1)

    def reach(side, way):
        return half - (side + way) % 2

    def remote(src, dst, send, recv, target):
        return pltpu.make_async_remote_copy(
            src_ref=src, dst_ref=dst, send_sem=send, recv_sem=recv,
            device_id=target, device_id_type=MESH,
        )

    def span(start, size, unit=ROWS):
        return pl.ds(start if isinstance(start, int) else pl.multiple_of(start, unit), size)

    def ring(matrix, side, way, hop, received=False, first=False):
        own, every = matrices[matrix]
        rows, cut = own.shape[0], own.shape[1] // 2
        apart = exclusive_rows(rows)
        keep = rows - apart
        columns = span(side * cut, cut, HD)
        shard = at(place + ways[way] * (hop if received else hop - 1))
        dst = every.at[span(shard * rows + parity * apart, keep), columns]
        src = own.at[span(parity * apart, keep), columns] if first else dst
        target = {"patch": left if way else right}
        flow = matrix * 4 + side * 2 + way
        return remote(src, dst, ring_send.at[flow, hop - 1], ring_recv.at[flow, hop - 1], target)

    def across(matrix, side, way, hop, received=False):
        own, every = matrices[matrix]
        rows, cut = own.shape[0], own.shape[1] // 2
        apart = exclusive_rows(rows)
        keep = rows - apart
        shard = at(place + ways[way] * hop)
        whose = 1 - parity if received else parity
        ref = every.at[span(shard * rows + whose * keep, apart), span(side * cut, cut, HD)]
        flow = matrix * 4 + side * 2 + way
        return remote(ref, ref, mate_send.at[flow, hop - 1], mate_recv.at[flow, hop - 1], {"groups": mate})

    def launch(matrix):
        for side in range(2):
            for way in range(2):
                ring(matrix, side, way, 1, first=True).start()

    def relay(matrix, step):
        hop, side = step // 2 + 1, step % 2
        for way in range(2):
            far = reach(side, way)

            def pass_on():
                ring(matrix, side, way, hop, received=True).wait_recv()
                when(hop < far, lambda: ring(matrix, side, way, hop + 1).start())
                across(matrix, side, way, hop).start()

            when(hop <= far, pass_on)

    def gathered(matrix):
        for side in range(2):
            for way in range(2):
                for hop in range(1, reach(side, way) + 1):
                    across(matrix, side, way, hop, True).wait_recv()
        own_copies[matrix].wait()

    pair = me + 1 - 2 * odd
    onward, behind = me + 2 - 4 * odd, me - 2 + 4 * odd
    has_onward = (onward >= 0) & (onward < n)
    has_behind = (behind >= 0) & (behind < n)

    def rim(leg, block, received=False):
        near, far = 2 * (1 - odd) * blocks + block, 2 * odd * blocks + block
        if received:
            dst = kvs.at[far if leg else near]
        else:
            dst = kvs.at[far]
        src = kvs.at[near] if leg else kv.at[block]
        return remote(
            src, dst, rim_send.at[leg, block], rim_recv.at[leg, block],
            {"patch": onward if leg else pair},
        )

    def rim_start():
        for block in range(blocks):
            rim(0, block).start()

    def rim_forward(block):
        rim(0, block, True).wait_recv()
        pl.when(has_onward)(lambda: rim(1, block).start())

    members = n // 2
    rank = lax.div(me, 2)
    first_owner = members // 2 - 1
    low, quarter = lead // 2, lead // 4

    def project_text():
        fetch_text.wait()
        conditioned = (
            rows_in[...].astype(jnp.float32) * (1.0 + row_mod[1:2, :]) + row_mod[0:1, :]
        ).astype(jnp.bfloat16)

        @pl.loop(0, part.shape[1] // TILE)
        def _(index):
            window = pl.ds(pl.multiple_of(index * TILE, TILE), TILE)
            part[:, window] = jnp.dot(
                conditioned, out[pl.ds(0, wt.shape[0]), window], preferred_element_type=jnp.float32
            ).astype(part.dtype)

    def text_swap():
        return remote(
            part.at[span((1 - odd) * low, low)], fetched, text_send.at[0], text_recv.at[0], {"patch": pair}
        )

    def contribute(piece, received=None):
        owner = 2 * (first_owner + piece) + odd
        slot = rank if received is None else received
        return remote(
            folded.at[pl.ds(piece * quarter, quarter)], sums.at[slot],
            sums_send.at[piece], sums_recv.at[slot], {"patch": owner},
        )

    def share(piece, member):
        ref = text.at[span(odd * low + piece * quarter, quarter)]
        return remote(ref, ref, share_send.at[member], share_recv.at[piece], {"patch": 2 * member + odd})

    def text_back():
        ref = text.at[span(odd * low, low)]
        return remote(ref, ref, text_send.at[1], text_recv.at[1], {"patch": pair})

    def text_start():
        project_text()
        text_swap().start()
        pl.when(section == 0)(fetch_state.wait)

    def text_fold():
        text_swap().wait_recv()
        folded[...] = (
            part[span(odd * low, low), :].astype(jnp.float32) + fetched[...].astype(jnp.float32)
        ).astype(folded.dtype)
        for piece in range(2):
            pl.when(rank != first_owner + piece)(lambda: contribute(piece).start())

    def text_reduce():
        for piece in range(2):
            owner = first_owner + piece

            @pl.when(rank == owner)
            def _():
                added = folded[pl.ds(piece * quarter, quarter), :].astype(jnp.float32)
                for member in range(members):
                    if member != owner:
                        contribute(piece, member).wait_recv()
                        added = added + sums[member].astype(jnp.float32)
                total[...] = added.astype(total.dtype)
                keep = pltpu.make_async_copy(
                    total, text.at[span(odd * low + piece * quarter, quarter)], text_sem.at[0]
                )
                keep.start()
                keep.wait()
                for member in range(members):
                    if member != owner:
                        share(piece, member).start()

    def text_spread():
        for piece in range(2):
            pl.when(rank != first_owner + piece)(lambda: share(piece, 0).wait_recv())
        text_back().start()

    def text_arrive():
        own = text.at[span((1 - odd) * low, low)]
        remote(own, own, text_send.at[1], text_recv.at[1], {"patch": pair}).wait_recv()

    def text_settle():
        text_swap().wait_send()
        text_back().wait_send()
        for piece in range(2):
            owner = first_owner + piece
            pl.when(rank != owner)(lambda: contribute(piece).wait_send())

            @pl.when(rank == owner)
            def _():
                for member in range(members):
                    if member != owner:
                        share(piece, member).wait_send()

    def norm(source, first, last):
        @pl.loop(first, last)
        def _(index):
            window = pl.ds(pl.multiple_of(index * ROWS, ROWS), ROWS)
            values = source[window, :].astype(jnp.float32)
            center = values - jnp.mean(values, axis=-1, keepdims=True)
            variance = jnp.mean(center * center, axis=-1, keepdims=True)
            scaled = center * lax.rsqrt(variance + EPSILON)
            normed[window, :] = (
                scaled * (1.0 + modulation[1:2, :]) + modulation[0:1, :]
            ).astype(normed.dtype)

    def project_query(after):
        @pl.loop(0, inner // TILE)
        def _(index):
            window = pl.ds(pl.multiple_of(index * TILE, TILE), TILE)
            query[:, window] = jnp.dot(
                normed[...], wq_all[:, window], preferred_element_type=jnp.float32
            ).astype(query.dtype)
            after(index)

    together = 4 if heads % 4 == 0 else 1
    bunches = heads // together

    def attend(after):
        @pl.loop(0, blocks * bunches)
        def _(index):
            block = lax.div(index, bunches)
            bunch = lax.rem(index, bunches)
            rows = pl.ds(pl.multiple_of(block * BLK, BLK), BLK)
            limit = lead + counts[block] * BLK
            live = lax.broadcasted_iota(jnp.int32, (BLK, keys), 1) < limit
            picks = [
                jnp.clip(chosen[block, slot] - (me - 1) * blocks, 0, 3 * blocks - 1)
                for slot in range(spread)
            ]
            for one in range(together):
                start = bunch * (together * HD) + one * HD
                columns = pl.ds(pl.multiple_of(start, HD), HD)
                beyond = pl.ds(pl.multiple_of(inner + start, HD), HD)
                key = jnp.concatenate([text[:, columns]] + [kvs[pick, :, columns] for pick in picks], axis=0)
                value = jnp.concatenate([text[:, beyond]] + [kvs[pick, :, beyond] for pick in picks], axis=0)
                scores = lax.dot_general(
                    query[rows, columns], key, (((1,), (1,)), ((), ())),
                    preferred_element_type=jnp.float32,
                )
                scores = jnp.where(live, scores, -1e30)
                peak = jnp.max(scores, axis=-1, keepdims=True)
                raised = jnp.exp((scores - peak) * HD ** (-0.5))
                whole = jnp.sum(raised, axis=-1, keepdims=True)
                share_of = jnp.dot(
                    raised.astype(jnp.bfloat16), value, preferred_element_type=jnp.float32
                )
                mixed[rows, columns] = (share_of / whole).astype(mixed.dtype)
            after(index)

    parts = width // (3 * TILE) if width % (3 * TILE) == 0 else 1
    part_width = width // parts

    def project_out(source, index_from, index_to):
        @pl.loop(index_from, index_to)
        def _(index):
            window = pl.ds(pl.multiple_of(index * TILE, TILE), TILE)
            projected = jnp.dot(mixed[...], wo_all[:, window], preferred_element_type=jnp.float32)
            out[:, window] = (
                source[:, window].astype(jnp.float32) + modulation[2:3, window] * projected
            ).astype(out.dtype)

    def hand(index):
        window = pl.ds(index * part_width, part_width)
        return remote(
            out.at[:, window], inbox.at[:, window],
            hand_send.at[index], hand_recv.at[index], {"section": 1 - section},
        )

    def wait_keys():
        own_copies[2].wait()
        for block in range(blocks):
            pl.when(has_behind)(lambda: rim(1, block, True).wait_recv())
        text_arrive()

    steps = 2 * half
    tiles = tokens // ROWS

    def open_gate(index):
        pl.semaphore_signal(gate.at[index], inc=1, device_id={"section": 1 - section}, device_id_type=MESH)

    each = part_width // TILE
    calls = inner // TILE

    def relay_at(pairs):
        def after(index):
            for when_index, step in pairs:
                pl.when(index == when_index)(lambda: relay(1, step))
        return after

    def finish(index):
        project_out(inbox, index * each, (index + 1) * each)

    actions = {
        "launch": launch,
        "copies": lambda: [copy.start() for copy in own_copies],
        "keys": lambda block: rim(0, block).start(),
        "forward": rim_forward,
        "text": text_start,
        "fold": text_fold,
        "reduce": text_reduce,
        "spread": text_spread,
        "norm": lambda index: norm(inbox, index * tiles // steps, (index + 1) * tiles // steps),
        "relay": relay,
        "open": open_gate,
        "pass": lambda index: pl.semaphore_wait(gate.at[index], 1),
        "query": lambda *pairs: (gathered(0), project_query(relay_at(pairs))),
        "attend": lambda *pairs: (wait_keys(), attend(relay_at(pairs))),
    }

    def play(script):
        for name, *values in script:
            actions[name](*values)

    @pl.when(section == 0)
    def _():
        fetch_text.start()
        fetch_state.start()
        play(script_first(steps, blocks))
        gathered(1)
        for index in range(parts):
            finish(index)
            hand(index).start()

    @pl.when(section == 1)
    def _():
        fetch_text.start()
        early, late = script_second(steps, blocks)
        play(early)
        for index in range(parts):
            hand(index).wait_recv()
        norm(inbox, 0, tiles)
        play(late)
        gathered(1)
        project_out(inbox, 0, width // TILE)

    for matrix in range(2):
        for side in range(2):
            for way in range(2):
                for hop in range(1, reach(side, way) + 1):
                    across(matrix, side, way, hop).wait_send()
                    ring(matrix, side, way, hop).wait_send()
    text_settle()
    for block in range(blocks):
        rim(0, block).wait_send()
        pl.when(has_onward)(lambda: rim(1, block).wait_send())

    @pl.when(section == 0)
    def _():
        for index in range(parts):
            hand(index).wait_send()


def run(n, chosen, counts, modulation, rows_in, row_mod, state, wq, wo, kv, wt):
    half = n // 2
    tokens, width = state.shape
    inner = wq.shape[1]
    lead = rows_in.shape[0]
    pairs = kv.shape[2]
    blocks = kv.shape[0]
    smem = pl.BlockSpec(memory_space=pltpu.SMEM)
    vmem = pl.BlockSpec(memory_space=pltpu.VMEM)
    anywhere = pl.BlockSpec(memory_space=pl.ANY)
    dma = pltpu.SemaphoreType.DMA
    parts = width // (3 * TILE) if width % (3 * TILE) == 0 else 1
    b16 = jnp.bfloat16
    return pl.pallas_call(
        functools.partial(kernel, n),
        out_shape=jax.ShapeDtypeStruct(state.shape, state.dtype),
        in_specs=[smem, smem] + [vmem] * 3 + [anywhere] * 5,
        out_specs=vmem,
        scratch_shapes=[
            pltpu.VMEM((n * wq.shape[0], inner), b16),
            pltpu.VMEM((n * wo.shape[0], width), b16),
            pltpu.VMEM((3 * blocks,) + kv.shape[1:], b16),
            pltpu.VMEM((lead, pairs), b16),
            pltpu.VMEM((lead, pairs), b16),
            pltpu.VMEM((lead // 2, pairs), b16),
            pltpu.VMEM((lead // 2, pairs), b16),
            pltpu.VMEM((half, lead // 4, pairs), b16),
            pltpu.VMEM((lead // 4, pairs), b16),
            pltpu.VMEM((tokens, width), b16),
            pltpu.VMEM((tokens, inner), b16),
            pltpu.VMEM((tokens, inner), b16),
            pltpu.VMEM((tokens, width), b16),
            dma((8, half)), dma((8, half)), dma((8, half)), dma((8, half)),
            dma((2, blocks)), dma((2, blocks)),
            dma((2,)), dma((2,)), dma((2,)), dma((half,)), dma((half,)), dma((2,)),
            dma((parts,)), dma((parts,)), dma((5,)), dma((1,)),
            pltpu.SemaphoreType.REGULAR((3,)),
        ],
        compiler_params=pltpu.CompilerParams(
            collective_id=0, has_side_effects=True, vmem_limit_bytes=60 * 2**20
        ),
        name="layers",
    )(chosen, counts, modulation, rows_in, row_mod, state, wq, wo, kv, wt)


def local(
    hidden_in, text_rows, mod_table, timestep, w_query, w_out, w_text, stale_kv, mask_blocks, counts
):
    patch_id = lax.axis_index("patch")
    n = lax.axis_size("patch")
    width = text_rows.shape[1]
    modulation = lax.dynamic_index_in_dim(mod_table, timestep[0], 0, keepdims=False)[0]
    row_mod = lax.dynamic_slice_in_dim(modulation[3:5], patch_id * width, width, 1)
    kv = stale_kv[0].reshape(-1, BLK, stale_kv.shape[2])
    result = run(
        n, mask_blocks, counts, modulation, text_rows, row_mod, hidden_in, w_query[0], w_out[0], kv, w_text[0]
    )
    return result[None]


def solution(mesh):
    in_specs = (
        P(("groups", "patch"), None),
        P("groups", "patch"),
        P(None, "section", None, None),
        P("groups"),
        P("section", "patch", None),
        P("section", "patch", None),
        P("section", "patch", None),
        P("section", ("groups", "patch"), None),
        P(("groups", "patch"), None),
        P(("groups", "patch")),
    )
    out_specs = P("section", ("groups", "patch"), None)
    return jax.shard_map(local, mesh=mesh, in_specs=in_specs, out_specs=out_specs, check_vma=False)
```

```python
import functools

import jax
import jax.numpy as jnp
from jax import lax
from jax.experimental import pallas as pl
from jax.experimental.pallas import tpu as pltpu
from jax.sharding import PartitionSpec as P

HD = 128
BLK = 128
EPSILON = 1e-06
MESH = pl.DeviceIdType.MESH
ROWS = 16


def exclusive_rows(rows, twelfths):
    return max(rows * twelfths // 12 // ROWS, 1) * ROWS


TILE = 256
GUESTS = 8
PHI = 5


def script_first(steps, blocks):
    sends, onward, text = (-1, 1, 3), (2, 4, 6), (1, 3, 5)
    out = [("launch", 0)] + [("launch", 1)]
    out += [("keys", b) for b in range(blocks) if sends[b] < 0] + [("copies",), ("text",)]
    for s in range(steps):
        out += [("norm", s), ("relay", 0, s)]
        if 0 and s == 2: out += [("launch", 1)]
        if s >= 0: out += [("relay", 1, s - 0)]
        out += [("keys", b) for b in range(blocks) if sends[b] == s]
        if s == text[0]: out += [("fold",)]
        out += [("forward", b) for b in range(blocks) if onward[b] == s]
        if s == text[1]: out += [("reduce",)]
        if s == text[2]: out += [("spread",)]
        if s == 6: out += [("open", 0)]
    rest = list(range(steps - 0, steps))
    out += [("query",) + tuple(zip((5,), rest)), ("attend",) + tuple(zip((2, 5, 8), rest[1:]))]
    return out


def script_second(steps, blocks):
    sends, onward, text = (-1, 1, 3), (2, 4, 6), (1, 3, 5)
    out = [("copies",), ("text",), ("pass", 0), ("launch", 0)]
    out += [("keys", b) for b in range(blocks) if sends[b] < 0]
    for s in range(steps):
        out += [("relay", 0, s)]
        if s == 2: out += [("launch", 1)]
        if s >= 4: out += [("relay", 1, s - 4)]
        out += [("keys", b) for b in range(blocks) if sends[b] == s]
        if s == text[0]: out += [("fold",)]
        out += [("forward", b) for b in range(blocks) if onward[b] == s]
        if s == text[1]: out += [("reduce",)]
        if s == text[2]: out += [("spread",)]
    rest = list(range(steps - 4, steps))
    return out, [("query",) + tuple(zip((5,), rest)), ("attend",) + tuple(zip((2, 5, 8), rest[1:]))]

def kernel(
    n, chosen, counts, modulation, rows_in, row_mod, state, wq, wo, kv, wt, final,
    wq_all, wo_all, kvs, text, part, fetched, folded, sums, total, normed, query, mixed, inbox, out, gathering, transit, guest, answer,
    ring_send, ring_recv, mate_send, mate_recv, rim_send, rim_recv, side_send, side_recv,
    inner_send, inner_recv, cross_send, cross_recv, inject_send, inject_recv, guest_send, guest_recv, back_send, back_recv,
    text_send, text_recv, sums_send, sums_recv, share_send, share_recv, hand_send, hand_recv, own_sem, text_sem, final_sem, gate,
):
    me = lax.axis_index("patch")
    group = lax.axis_index("groups")
    section = lax.axis_index("section")
    parity = lax.rem(group, 2)
    mate = group + 1 - 2 * parity
    half = n // 2
    odd = lax.rem(me, 2)
    place = (1 - odd) * lax.div(me, 2) + odd * (n - 1 - lax.div(me, 2))
    tokens, width = state.shape
    inner = query.shape[1]
    heads = inner // HD
    blocks = kv.shape[0]
    spread = chosen.shape[1]
    lead = text.shape[0]
    keys = lead + spread * BLK

    def at(position):
        position = lax.rem(position + n, n)
        high = lax.div(position, half)
        return (1 - high) * 2 * position + high * (2 * (n - 1 - position) + 1)

    def when(condition, action):
        if isinstance(condition, bool):
            if condition:
                action()
        else:
            pl.when(condition)(action)

    right, left = at(place + 1), at(place - 1)

    own_copies = [
        pltpu.make_async_copy(wq, wq_all.at[pl.ds(pl.multiple_of(me * wq.shape[0], ROWS), wq.shape[0])], own_sem.at[0]),
        pltpu.make_async_copy(wo, wo_all.at[pl.ds(pl.multiple_of(me * wo.shape[0], ROWS), wo.shape[0])], own_sem.at[1]),
        pltpu.make_async_copy(kv, kvs.at[pl.ds(blocks, blocks)], own_sem.at[2]),
    ]
    fetch_text = pltpu.make_async_copy(wt, out.at[pl.ds(0, wt.shape[0])], own_sem.at[3])
    fetch_state = pltpu.make_async_copy(state, inbox, own_sem.at[4])

    barrier = pltpu.get_barrier_semaphore()
    for step in range(1, n):
        pl.semaphore_signal(barrier, inc=1, device_id={"patch": lax.rem(me + step, n)}, device_id_type=MESH)
    pl.semaphore_signal(barrier, inc=1, device_id={"groups": mate}, device_id_type=MESH)
    pl.semaphore_signal(barrier, inc=1, device_id={"section": 1 - section}, device_id_type=MESH)
    pl.semaphore_wait(barrier, n + 1)

    matrices = ((wq, wq_all), (wo, wo_all))
    ways = (-1, 1)

    def reach(side, way):
        return half - (side + way) % 2

    def remote(src, dst, send, recv, target):
        return pltpu.make_async_remote_copy(
            src_ref=src, dst_ref=dst, send_sem=send, recv_sem=recv,
            device_id=target, device_id_type=MESH,
        )

    def span(start, size, unit=ROWS):
        return pl.ds(start if isinstance(start, int) else pl.multiple_of(start, unit), size)

    def ring(matrix, side, way, hop, received=False, first=False):
        own, every = matrices[matrix]
        rows, cut = own.shape[0], own.shape[1] // 2
        apart = exclusive_rows(rows, 5 if matrix else 6)
        keep = rows - apart
        columns = span(side * cut, cut, HD)
        shard = at(place + ways[way] * (hop if received else hop - 1))
        dst = every.at[span(shard * rows + parity * apart, keep), columns]
        src = own.at[span(parity * apart, keep), columns] if first else dst
        target = {"patch": left if way else right}
        flow = matrix * 4 + side * 2 + way
        return remote(src, dst, ring_send.at[flow, hop - 1], ring_recv.at[flow, hop - 1], target)

    def across(matrix, side, way, hop, received=False):
        own, every = matrices[matrix]
        rows, cut = own.shape[0], own.shape[1] // 2
        apart = exclusive_rows(rows, 5 if matrix else 6)
        keep = rows - apart
        shard = at(place + ways[way] * hop)
        whose = 1 - parity if received else parity
        ref = every.at[span(shard * rows + whose * keep, apart), span(side * cut, cut, HD)]
        flow = matrix * 4 + side * 2 + way
        return remote(ref, ref, mate_send.at[flow, hop - 1], mate_recv.at[flow, hop - 1], {"groups": mate})

    def launch(matrix):
        for side in range(2):
            for way in range(2):
                ring(matrix, side, way, 1, first=True).start()

    def relay(matrix, step):
        hop, side = step // 2 + 1, step % 2
        for way in range(2):
            far = reach(side, way)

            def pass_on():
                ring(matrix, side, way, hop, received=True).wait_recv()
                when(hop < far, lambda: ring(matrix, side, way, hop + 1).start())
                across(matrix, side, way, hop).start()

            when(hop <= far, pass_on)

    def gathered(matrix):
        for side in range(2):
            for way in range(2):
                for hop in range(1, reach(side, way) + 1):
                    across(matrix, side, way, hop, True).wait_recv()
        own_copies[matrix].wait()

    pair = me + 1 - 2 * odd
    onward, behind = me + 2 - 4 * odd, me - 2 + 4 * odd
    has_onward = (onward >= 0) & (onward < n)
    has_behind = (behind >= 0) & (behind < n)

    members = n // 2
    rank = lax.div(me, 2)

    def inside(device):
        return (device >= 2) & (device < n - 2)

    mid = inside(me)

    def rim(leg, block, received=False, keys_only=False):
        near, far = 2 * (1 - odd) * blocks + block, 2 * odd * blocks + block
        width_of = pl.ds(0, inner if keys_only else 2 * inner)
        if received:
            dst = kvs.at[far if leg else near, :, width_of]
        else:
            dst = kvs.at[far, :, width_of]
        src = kvs.at[near, :, width_of] if leg else kv.at[block]
        return remote(
            src, dst, rim_send.at[leg, block], rim_recv.at[leg, block],
            {"patch": onward if leg else pair},
        )

    def detour(leg, block, received=False):
        values = pl.ds(inner, inner)
        if leg:
            slot = (2 * odd if received else 2 * (1 - odd)) * blocks + block
            src, dst, target = transit.at[block], kvs.at[slot, :, values], pair
        else:
            src, dst, target = kv.at[block, :, values], transit.at[block], behind
        return remote(src, dst, side_send.at[leg, block], side_recv.at[leg, block], {"patch": target})

    def rim_start(block):
        rim(0, block).start()
        pl.when(has_behind & inside(behind))(lambda: detour(0, block).start())

    def rim_forward(block):
        rim(0, block, True).wait_recv()
        pl.when(has_onward & inside(onward))(lambda: rim(1, block, keys_only=True).start())
        pl.when(has_onward & jnp.logical_not(inside(onward)))(lambda: rim(1, block).start())

        @pl.when(mid)
        def _():
            detour(0, block, True).wait_recv()
            detour(1, block).start()

    def rim_arrive(block):
        pl.when(has_behind & jnp.logical_not(mid))(lambda: rim(1, block, True).wait_recv())

        @pl.when(mid)
        def _():
            rim(1, block, True, keys_only=True).wait_recv()
            detour(1, block, True).wait_recv()

    def rim_settle(block):
        rim(0, block).wait_send()
        pl.when(has_onward & inside(onward))(lambda: rim(1, block, keys_only=True).wait_send())
        pl.when(has_onward & jnp.logical_not(inside(onward)))(lambda: rim(1, block).wait_send())
        pl.when(has_behind & inside(behind))(lambda: detour(0, block).wait_send())
        pl.when(mid)(lambda: detour(1, block).wait_send())

    first_owner = members // 2 - 1
    low, quarter = lead // 2, lead // 4

    def project_text():
        fetch_text.wait()
        conditioned = (
            rows_in[...].astype(jnp.float32) * (1.0 + row_mod[1:2, :]) + row_mod[0:1, :]
        ).astype(jnp.bfloat16)

        @pl.loop(0, part.shape[1] // TILE)
        def _(index):
            window = pl.ds(pl.multiple_of(index * TILE, TILE), TILE)
            part[:, window] = jnp.dot(
                conditioned, out[pl.ds(0, wt.shape[0]), window], preferred_element_type=jnp.float32
            ).astype(part.dtype)

    def text_swap():
        return remote(
            part.at[span((1 - odd) * low, low)], fetched, text_send.at[0], text_recv.at[0], {"patch": pair}
        )

    def contribute(piece, received=None):
        owner = 2 * (first_owner + piece) + odd
        slot = rank if received is None else received
        return remote(
            folded.at[pl.ds(piece * quarter, quarter)], sums.at[slot],
            sums_send.at[piece], sums_recv.at[slot], {"patch": owner},
        )

    def share(piece, member):
        ref = text.at[span(odd * low + piece * quarter, quarter)]
        return remote(ref, ref, share_send.at[member], share_recv.at[piece], {"patch": 2 * member + odd})

    def text_back():
        ref = text.at[span(odd * low, low)]
        return remote(ref, ref, text_send.at[1], text_recv.at[1], {"patch": pair})

    def text_start():
        project_text()
        text_swap().start()
        pl.when(section == 0)(fetch_state.wait)

    def text_fold():
        text_swap().wait_recv()
        folded[...] = (
            part[span(odd * low, low), :].astype(jnp.float32) + fetched[...].astype(jnp.float32)
        ).astype(folded.dtype)
        for piece in range(2):
            pl.when(rank != first_owner + piece)(lambda: contribute(piece).start())

    def text_reduce():
        for piece in range(2):
            owner = first_owner + piece

            @pl.when(rank == owner)
            def _():
                added = folded[pl.ds(piece * quarter, quarter), :].astype(jnp.float32)
                for member in range(members):
                    if member != owner:
                        contribute(piece, member).wait_recv()
                        added = added + sums[member].astype(jnp.float32)
                total[...] = added.astype(total.dtype)
                keep = pltpu.make_async_copy(
                    total, text.at[span(odd * low + piece * quarter, quarter)], text_sem.at[0]
                )
                keep.start()
                keep.wait()
                for member in range(members):
                    if member != owner:
                        share(piece, member).start()

    def text_spread():
        for piece in range(2):
            pl.when(rank != first_owner + piece)(lambda: share(piece, 0).wait_recv())
        text_back().start()

    def text_arrive():
        own = text.at[span((1 - odd) * low, low)]
        remote(own, own, text_send.at[1], text_recv.at[1], {"patch": pair}).wait_recv()

    def text_settle():
        text_swap().wait_send()
        text_back().wait_send()
        for piece in range(2):
            owner = first_owner + piece
            pl.when(rank != owner)(lambda: contribute(piece).wait_send())

            @pl.when(rank == owner)
            def _():
                for member in range(members):
                    if member != owner:
                        share(piece, member).wait_send()

    def norm(source, first, last):
        @pl.loop(first, last)
        def _(index):
            window = pl.ds(pl.multiple_of(index * ROWS, ROWS), ROWS)
            values = source[window, :].astype(jnp.float32)
            center = values - jnp.mean(values, axis=-1, keepdims=True)
            variance = jnp.mean(center * center, axis=-1, keepdims=True)
            scaled = center * lax.rsqrt(variance + EPSILON)
            normed[window, :] = (
                scaled * (1.0 + modulation[1:2, :]) + modulation[0:1, :]
            ).astype(normed.dtype)

    def project_query(after):
        @pl.loop(0, inner // TILE)
        def _(index):
            window = pl.ds(pl.multiple_of(index * TILE, TILE), TILE)
            query[:, window] = jnp.dot(
                normed[...], wq_all[:, window], preferred_element_type=jnp.float32
            ).astype(query.dtype)
            after(index)

    together = 4 if heads % 4 == 0 else 1
    bunches = heads // together

    def attend(after):
        @pl.loop(0, blocks * bunches)
        def _(index):
            block = lax.div(index, bunches)
            bunch = lax.rem(index, bunches)
            rows = pl.ds(pl.multiple_of(block * BLK, BLK), BLK)
            limit = lead + counts[block] * BLK
            live = lax.broadcasted_iota(jnp.int32, (BLK, keys), 1) < limit
            picks = [
                jnp.clip(chosen[block, slot] - (me - 1) * blocks, 0, 3 * blocks - 1)
                for slot in range(spread)
            ]
            for one in range(together):
                start = bunch * (together * HD) + one * HD
                columns = pl.ds(pl.multiple_of(start, HD), HD)
                beyond = pl.ds(pl.multiple_of(inner + start, HD), HD)
                key = jnp.concatenate([text[:, columns]] + [kvs[pick, :, columns] for pick in picks], axis=0)
                value = jnp.concatenate([text[:, beyond]] + [kvs[pick, :, beyond] for pick in picks], axis=0)
                scores = lax.dot_general(
                    query[rows, columns], key, (((1,), (1,)), ((), ())),
                    preferred_element_type=jnp.float32,
                )
                scores = jnp.where(live, scores, -1e30)
                peak = jnp.max(scores, axis=-1, keepdims=True)
                raised = jnp.exp((scores - peak) * HD ** (-0.5))
                whole = jnp.sum(raised, axis=-1, keepdims=True)
                share_of = jnp.dot(
                    raised.astype(jnp.bfloat16), value, preferred_element_type=jnp.float32
                )
                mixed[rows, columns] = (share_of / whole).astype(mixed.dtype)
            after(index)

    parts = width // (3 * TILE) if width % (3 * TILE) == 0 else 1
    part_width = width // parts

    def project_out(source, index_from, index_to):
        @pl.loop(index_from, index_to)
        def _(index):
            window = pl.ds(pl.multiple_of(index * TILE, TILE), TILE)
            projected = jnp.dot(mixed[...], wo_all[:, window], preferred_element_type=jnp.float32)
            out[:, window] = (
                source[:, window].astype(jnp.float32) + modulation[2:3, window] * projected
            ).astype(out.dtype)

    def hand(index):
        window = pl.ds(index * part_width, part_width)
        return remote(
            out.at[:, window], inbox.at[:, window],
            hand_send.at[index], hand_recv.at[index], {"section": 1 - section},
        )

    def store(index):
        window = pl.ds(index * part_width, part_width)
        return pltpu.make_async_copy(out.at[:, window], final.at[:, window], final_sem.at[index])

    def wait_keys():
        own_copies[2].wait()
        for block in range(blocks):
            rim_arrive(block)
        text_arrive()

    steps = 2 * half
    tiles = tokens // ROWS

    def open_gate(index):
        pl.semaphore_signal(gate.at[index], inc=1, device_id={"section": 1 - section}, device_id_type=MESH)

    each = part_width // TILE
    calls = inner // TILE

    def relay_at(pairs):
        def after(index):
            for when_index, step in pairs:
                pl.when(index == when_index)(lambda: relay(1, step))
        return after

    strip = 2 * wo.shape[0]
    split = strip % HD == 0 and half > 1

    def gathered_near(last):
        for side in range(2):
            for way in range(2):
                far = reach(side, way)
                for hop in range(1, far + 1):
                    if (hop == half) == last:
                        across(1, side, way, hop, True).wait_recv()
        if not last:
            own_copies[1].wait()

    def project_near():
        far_strip = lax.div(at(place + half), 2)

        @pl.loop(0, width // TILE)
        def _(index):
            window = pl.ds(pl.multiple_of(index * TILE, TILE), TILE)
            partial = None
            for other in range(1, members):
                strip_at = pl.multiple_of(lax.rem(far_strip + other, members) * strip, HD)
                term = jnp.dot(
                    mixed[:, pl.ds(strip_at, strip)], wo_all[pl.ds(strip_at, strip), window],
                    preferred_element_type=jnp.float32,
                )
                partial = term if partial is None else partial + term
            gathering[:, window] = inbox[:, window].astype(jnp.float32) + modulation[2:3, window] * partial

    def project_far(index_from, index_to):
        strip_at = pl.multiple_of(lax.div(at(place + half), 2) * strip, HD)

        @pl.loop(index_from, index_to)
        def _(index):
            window = pl.ds(pl.multiple_of(index * TILE, TILE), TILE)
            term = jnp.dot(
                mixed[:, pl.ds(strip_at, strip)], wo_all[pl.ds(strip_at, strip), window],
                preferred_element_type=jnp.float32,
            )
            out[:, window] = (gathering[:, window] + modulation[2:3, window] * term).astype(out.dtype)

    edge = members == 4
    ring_size = n - 4
    ring_half = ring_size // 2
    spot = (1 - odd) * (rank - 1) + odd * (ring_size - rank)

    def inner_at(position):
        position = lax.rem(position + ring_size, ring_size)
        high = lax.div(position, ring_half)
        return 2 + (1 - high) * 2 * position + high * (2 * (ring_size - 1 - position) + 1)

    def partner_of(device):
        return device + 2 - 4 * lax.rem(lax.div(device, 2), 2)

    partner = partner_of(me)
    inner_rows = wq.shape[0]
    inner_apart = exclusive_rows(inner_rows, PHI)
    inner_keep = inner_rows - inner_apart
    inner_cut = wq.shape[1] // 2

    def inner_reach(kind, side, way):
        return ring_half - (kind + side + way) % 2

    def inner_piece(device, side, every=True):
        start = (device * inner_rows if every else 0) + parity * inner_apart
        return (wq_all if every else wq).at[span(start, inner_keep), pl.ds(side * inner_cut, inner_cut)]

    def inner_ring(kind, side, way, hop, received=False):
        home = inner_at(spot + ways[way] * (hop if received else hop - 1))
        dst = inner_piece(partner_of(home) if kind else home, side)
        src = inner_piece(me, side, False) if hop == 1 and not kind and not received else dst
        target = inner_at(spot - 1) if way else inner_at(spot + 1)
        flow = kind * 4 + side * 2 + way
        return remote(src, dst, inner_send.at[flow, hop - 1], inner_recv.at[flow, hop - 1], {"patch": target})

    def inner_across(kind, side, way, hop, received=False):
        home = inner_at(spot + ways[way] * hop)
        shard = partner_of(home) if kind else home
        whose = 1 - parity if received else parity
        ref = wq_all.at[
            span(shard * inner_rows + whose * inner_keep, inner_apart), pl.ds(side * inner_cut, inner_cut)
        ]
        flow = kind * 4 + side * 2 + way
        return remote(ref, ref, cross_send.at[flow, hop], cross_recv.at[flow, hop], {"groups": mate})

    def inject(side, received=False):
        dst = inner_piece(partner if received else me, side)
        return remote(
            inner_piece(me, side, False), dst, inject_send.at[side], inject_recv.at[side], {"patch": partner}
        )

    def inner_launch():
        @pl.when(mid)
        def _():
            for side in range(2):
                for way in range(2):
                    inner_ring(0, side, way, 1).start()

        @pl.when(jnp.logical_not(mid))
        def _():
            for side in range(2):
                inject(side).start()

    def inner_pass(kind, side, hop):
        for way in range(2):
            far = inner_reach(kind, side, way)
            if hop <= far:
                inner_ring(kind, side, way, hop, received=True).wait_recv()
                if hop < far:
                    inner_ring(kind, side, way, hop + 1).start()
                inner_across(kind, side, way, hop).start()

    def inner_relay(step):
        turn, side = step // 2, step % 2
        if turn > 3:
            return

        @pl.when(mid)
        def _():
            if turn == 0:
                inject(side, True).wait_recv()
                for way in range(2):
                    inner_ring(1, side, way, 1).start()
                inner_across(1, side, 0, 0).start()
            inner_pass(turn % 2, side, turn // 2 + 1)

    def inner_messages():
        for kind in range(2):
            for side in range(2):
                for way in range(2):
                    for hop in range(1, inner_reach(kind, side, way) + 1):
                        yield kind, side, way, hop

    def guest_part(index):
        share_of = tokens // GUESTS
        window = pl.ds(index * share_of, share_of)
        return remote(
            normed.at[window], guest.at[window], guest_send.at[index], guest_recv.at[index], {"patch": partner}
        )

    def give_back(index):
        window = pl.ds(index * TILE if isinstance(index, int) else pl.multiple_of(index * TILE, TILE), TILE)
        return remote(
            answer.at[:, window], query.at[:, window], back_send.at[index], back_recv.at[index], {"patch": partner}
        )

    def inner_norm(step):
        if step < GUESTS:
            norm(inbox, step * tiles // GUESTS, (step + 1) * tiles // GUESTS)
            pl.when(jnp.logical_not(mid))(lambda: guest_part(step).start())

    def inner_query(*pairs):
        own_copies[0].wait()

        @pl.when(mid)
        def _():
            for side in range(2):
                inner_across(1, side, 0, 0, True).wait_recv()
            for message in inner_messages():
                inner_across(*message, received=True).wait_recv()
            for index in range(GUESTS):
                guest_part(index).wait_recv()

            @pl.loop(0, calls)
            def _(index):
                window = pl.ds(pl.multiple_of(index * TILE, TILE), TILE)
                answer[:, window] = jnp.dot(
                    guest[...], wq_all[:, window], preferred_element_type=jnp.float32
                ).astype(answer.dtype)
                give_back(index).start()

            project_query(relay_at(pairs))

        @pl.when(jnp.logical_not(mid))
        def _():
            for _, step in pairs:
                relay(1, step)
            for index in range(calls):
                give_back(index).wait_recv()

    def inner_settle():
        @pl.when(mid)
        def _():
            for side in range(2):
                inner_across(1, side, 0, 0).wait_send()
            for message in inner_messages():
                inner_across(*message).wait_send()
                inner_ring(*message).wait_send()
            for index in range(calls):
                give_back(index).wait_send()

        @pl.when(jnp.logical_not(mid))
        def _():
            for side in range(2):
                inject(side).wait_send()
            for index in range(GUESTS):
                guest_part(index).wait_send()

    def finish(index):
        project_out(inbox, index * each, (index + 1) * each)

    actions = {
        "launch": launch,
        "copies": lambda: [copy.start() for copy in own_copies],
        "keys": rim_start,
        "forward": rim_forward,
        "text": text_start,
        "fold": text_fold,
        "reduce": text_reduce,
        "spread": text_spread,
        "norm": lambda index: norm(inbox, index * tiles // steps, (index + 1) * tiles // steps),
        "relay": relay,
        "open": open_gate,
        "pass": lambda index: pl.semaphore_wait(gate.at[index], 1),
        "query": lambda *pairs: (gathered(0), project_query(relay_at(pairs))),
        "attend": lambda *pairs: (wait_keys(), attend(relay_at(pairs))),
    }

    inner_actions = {
        "launch": lambda matrix: launch(1) if matrix else inner_launch(),
        "norm": inner_norm,
        "relay": lambda matrix, step: relay(1, step) if matrix else inner_relay(step),
        "query": inner_query,
    }

    def play(script, own={}):
        for name, *values in script:
            own.get(name, actions[name])(*values)

    @pl.when(section == 0)
    def _():
        fetch_text.start()
        fetch_state.start()
        play(script_first(steps, blocks), inner_actions if edge else {})
        gathered(1)
        for index in range(parts):
            finish(index)
            hand(index).start()
            store(index).start()

    @pl.when(section == 1)
    def _():
        fetch_text.start()
        early, late = script_second(steps, blocks)
        play(early)
        for index in range(parts):
            hand(index).wait_recv()
        norm(inbox, 0, tiles)
        play(late)
        if split:
            gathered_near(False)
            project_near()
            gathered_near(True)
        else:
            gathered(1)
        for index in range(parts):
            if split:
                project_far(index * each, (index + 1) * each)
            else:
                finish(index)
            store(index).start()

    def settle(matrix):
        for side in range(2):
            for way in range(2):
                for hop in range(1, reach(side, way) + 1):
                    across(matrix, side, way, hop).wait_send()
                    ring(matrix, side, way, hop).wait_send()

    if edge:
        pl.when(section == 0)(inner_settle)
        pl.when(section == 1)(lambda: settle(0))
    else:
        settle(0)
    settle(1)
    text_settle()
    for block in range(blocks):
        rim_settle(block)

    for index in range(parts):
        store(index).wait()

    @pl.when(section == 0)
    def _():
        for index in range(parts):
            hand(index).wait_send()


def run(n, chosen, counts, modulation, rows_in, row_mod, state, wq, wo, kv, wt):
    half = n // 2
    tokens, width = state.shape
    inner = wq.shape[1]
    lead = rows_in.shape[0]
    pairs = kv.shape[2]
    blocks = kv.shape[0]
    smem = pl.BlockSpec(memory_space=pltpu.SMEM)
    vmem = pl.BlockSpec(memory_space=pltpu.VMEM)
    anywhere = pl.BlockSpec(memory_space=pl.ANY)
    dma = pltpu.SemaphoreType.DMA
    parts = width // (3 * TILE) if width % (3 * TILE) == 0 else 1
    b16 = jnp.bfloat16
    return pl.pallas_call(
        functools.partial(kernel, n),
        out_shape=jax.ShapeDtypeStruct(state.shape, state.dtype),
        in_specs=[smem, smem] + [vmem] * 3 + [anywhere] * 5,
        out_specs=anywhere,
        scratch_shapes=[
            pltpu.VMEM((n * wq.shape[0], inner), b16),
            pltpu.VMEM((n * wo.shape[0], width), b16),
            pltpu.VMEM((3 * blocks,) + kv.shape[1:], b16),
            pltpu.VMEM((lead, pairs), b16),
            pltpu.VMEM((lead, pairs), b16),
            pltpu.VMEM((lead // 2, pairs), b16),
            pltpu.VMEM((lead // 2, pairs), b16),
            pltpu.VMEM((half, lead // 4, pairs), b16),
            pltpu.VMEM((lead // 4, pairs), b16),
            pltpu.VMEM((tokens, width), b16),
            pltpu.VMEM((tokens, inner), b16),
            pltpu.VMEM((tokens, inner), b16),
            pltpu.VMEM((tokens, width), b16),
            pltpu.VMEM((tokens, width), b16),
            pltpu.VMEM((tokens, width), jnp.float32),
            pltpu.VMEM((blocks, BLK, inner), b16),
            pltpu.VMEM((tokens, width), b16),
            pltpu.VMEM((tokens, inner), b16),
            dma((8, half)), dma((8, half)), dma((8, half)), dma((8, half)),
            dma((2, blocks)), dma((2, blocks)), dma((2, blocks)), dma((2, blocks)),
            dma((8, 2)), dma((8, 2)), dma((8, 3)), dma((8, 3)), dma((2,)), dma((2,)), dma((GUESTS,)), dma((GUESTS,)),
            dma((inner // TILE,)), dma((inner // TILE,)),
            dma((2,)), dma((2,)), dma((2,)), dma((half,)), dma((half,)), dma((2,)),
            dma((parts,)), dma((parts,)), dma((5,)), dma((1,)), dma((parts,)),
            pltpu.SemaphoreType.REGULAR((3,)),
        ],
        compiler_params=pltpu.CompilerParams(
            collective_id=0, has_side_effects=True, vmem_limit_bytes=60 * 2**20
        ),
        name="layers",
    )(chosen, counts, modulation, rows_in, row_mod, state, wq, wo, kv, wt)


def local(
    hidden_in, text_rows, mod_table, timestep, w_query, w_out, w_text, stale_kv, mask_blocks, counts
):
    patch_id = lax.axis_index("patch")
    n = lax.axis_size("patch")
    width = text_rows.shape[1]
    modulation = lax.dynamic_index_in_dim(mod_table, timestep[0], 0, keepdims=False)[0]
    row_mod = lax.dynamic_slice_in_dim(modulation[3:5], patch_id * width, width, 1)
    kv = stale_kv[0].reshape(-1, BLK, stale_kv.shape[2])
    result = run(
        n, mask_blocks, counts, modulation, text_rows, row_mod, hidden_in, w_query[0], w_out[0], kv, w_text[0]
    )
    return result[None]


def solution(mesh):
    in_specs = (
        P(("groups", "patch"), None),
        P("groups", "patch"),
        P(None, "section", None, None),
        P("groups"),
        P("section", "patch", None),
        P("section", "patch", None),
        P("section", "patch", None),
        P("section", ("groups", "patch"), None),
        P(("groups", "patch"), None),
        P(("groups", "patch")),
    )
    out_specs = P("section", ("groups", "patch"), None)
    return jax.shard_map(local, mesh=mesh, in_specs=in_specs, out_specs=out_specs, check_vma=False)
```

```python
import functools

import jax
import jax.numpy as jnp
from jax import lax
from jax.experimental import pallas as pl
from jax.experimental.pallas import tpu as pltpu
from jax.sharding import PartitionSpec as P

HD = 128
BLK = 128
EPSILON = 1e-06
MESH = pl.DeviceIdType.MESH
ROWS = 16


def exclusive_rows(rows, twelfths):
    return max(rows * twelfths // 12 // ROWS, 1) * ROWS


TILE = 256
GUESTS = 8
PHI = 5


def script_first(steps, blocks):
    sends, onward, text = (-1, 1, 3), (2, 4, 6), (1, 3, 5)
    out = [("launch", 0)] + [("launch", 1)]
    out += [("keys", b) for b in range(blocks) if sends[b] < 0] + [("copies",), ("text",)]
    for s in range(steps):
        out += [("norm", s), ("relay", 0, s)]
        if 0 and s == 2: out += [("launch", 1)]
        if s >= 0: out += [("relay", 1, s - 0)]
        out += [("keys", b) for b in range(blocks) if sends[b] == s]
        if s == text[0]: out += [("fold",)]
        out += [("forward", b) for b in range(blocks) if onward[b] == s]
        if s == text[1]: out += [("reduce",)]
        if s == text[2]: out += [("spread",)]
        if s == 6: out += [("open", 0)]
    rest = list(range(steps - 0, steps))
    out += [("query",) + tuple(zip((5,), rest)), ("attend",) + tuple(zip((2, 5, 8), rest[1:]))]
    return out


def script_second(steps, blocks):
    sends, onward, text = (0, 2, 4), (2, 4, 6), (1, 3, 5)
    out = [("copies",), ("text",), ("pass", 0), ("launch", 0)]
    out += [("keys", b) for b in range(blocks) if sends[b] < 0]
    for s in range(steps):
        out += [("relay", 0, s)]
        if s == 2: out += [("launch", 1)]
        if s >= 4: out += [("relay", 1, s - 4)]
        out += [("keys", b) for b in range(blocks) if sends[b] == s]
        if s == text[0]: out += [("fold",)]
        out += [("forward", b) for b in range(blocks) if onward[b] == s]
        if s == text[1]: out += [("reduce",)]
        if s == text[2]: out += [("spread",)]
    rest = list(range(steps - 4, steps))
    return out, [("query",) + tuple(zip((5,), rest)), ("attend",) + tuple(zip((2, 5, 8), rest[1:]))]

def kernel(
    n, chosen, counts, modulation, rows_in, row_mod, state, wq, wo, kv, wt, final,
    wq_all, wo_all, kvs, text, part, fetched, folded, sums, total, normed, query, mixed, inbox, out, gathering, transit, guest, answer,
    ring_send, ring_recv, mate_send, mate_recv, rim_send, rim_recv, side_send, side_recv,
    inner_send, inner_recv, cross_send, cross_recv, inject_send, inject_recv, guest_send, guest_recv, back_send, back_recv,
    text_send, text_recv, sums_send, sums_recv, share_send, share_recv, hand_send, hand_recv, own_sem, text_sem, final_sem, gate,
):
    me = lax.axis_index("patch")
    group = lax.axis_index("groups")
    section = lax.axis_index("section")
    parity = lax.rem(group, 2)
    mate = group + 1 - 2 * parity
    half = n // 2
    odd = lax.rem(me, 2)
    place = (1 - odd) * lax.div(me, 2) + odd * (n - 1 - lax.div(me, 2))
    tokens, width = state.shape
    inner = query.shape[1]
    heads = inner // HD
    blocks = kv.shape[0]
    spread = chosen.shape[1]
    lead = text.shape[0]
    keys = lead + spread * BLK

    def at(position):
        position = lax.rem(position + n, n)
        high = lax.div(position, half)
        return (1 - high) * 2 * position + high * (2 * (n - 1 - position) + 1)

    def when(condition, action):
        if isinstance(condition, bool):
            if condition:
                action()
        else:
            pl.when(condition)(action)

    right, left = at(place + 1), at(place - 1)

    own_copies = [
        pltpu.make_async_copy(wq, wq_all.at[pl.ds(pl.multiple_of(me * wq.shape[0], ROWS), wq.shape[0])], own_sem.at[0]),
        pltpu.make_async_copy(wo, wo_all.at[pl.ds(pl.multiple_of(me * wo.shape[0], ROWS), wo.shape[0])], own_sem.at[1]),
        pltpu.make_async_copy(kv, kvs.at[pl.ds(blocks, blocks)], own_sem.at[2]),
    ]
    fetch_text = pltpu.make_async_copy(wt, out.at[pl.ds(0, wt.shape[0])], own_sem.at[3])
    fetch_state = pltpu.make_async_copy(state, inbox, own_sem.at[4])

    barrier = pltpu.get_barrier_semaphore()
    for step in range(1, n):
        pl.semaphore_signal(barrier, inc=1, device_id={"patch": lax.rem(me + step, n)}, device_id_type=MESH)
    pl.semaphore_signal(barrier, inc=1, device_id={"groups": mate}, device_id_type=MESH)
    pl.semaphore_signal(barrier, inc=1, device_id={"section": 1 - section}, device_id_type=MESH)
    pl.semaphore_wait(barrier, n + 1)

    matrices = ((wq, wq_all), (wo, wo_all))
    ways = (-1, 1)

    def reach(side, way):
        return half - (side + way) % 2

    def remote(src, dst, send, recv, target):
        return pltpu.make_async_remote_copy(
            src_ref=src, dst_ref=dst, send_sem=send, recv_sem=recv,
            device_id=target, device_id_type=MESH,
        )

    def span(start, size, unit=ROWS):
        return pl.ds(start if isinstance(start, int) else pl.multiple_of(start, unit), size)

    def ring(matrix, side, way, hop, received=False, first=False):
        own, every = matrices[matrix]
        rows, cut = own.shape[0], own.shape[1] // 2
        apart = exclusive_rows(rows, 5 if matrix else 6)
        keep = rows - apart
        columns = span(side * cut, cut, HD)
        shard = at(place + ways[way] * (hop if received else hop - 1))
        dst = every.at[span(shard * rows + parity * apart, keep), columns]
        src = own.at[span(parity * apart, keep), columns] if first else dst
        target = {"patch": left if way else right}
        flow = matrix * 4 + side * 2 + way
        return remote(src, dst, ring_send.at[flow, hop - 1], ring_recv.at[flow, hop - 1], target)

    def across(matrix, side, way, hop, received=False):
        own, every = matrices[matrix]
        rows, cut = own.shape[0], own.shape[1] // 2
        apart = exclusive_rows(rows, 5 if matrix else 6)
        keep = rows - apart
        shard = at(place + ways[way] * hop)
        whose = 1 - parity if received else parity
        ref = every.at[span(shard * rows + whose * keep, apart), span(side * cut, cut, HD)]
        flow = matrix * 4 + side * 2 + way
        return remote(ref, ref, mate_send.at[flow, hop - 1], mate_recv.at[flow, hop - 1], {"groups": mate})

    def launch(matrix):
        for side in range(2):
            for way in range(2):
                ring(matrix, side, way, 1, first=True).start()

    def relay(matrix, step):
        hop, side = step // 2 + 1, step % 2
        for way in range(2):
            far = reach(side, way)

            def pass_on():
                ring(matrix, side, way, hop, received=True).wait_recv()
                when(hop < far, lambda: ring(matrix, side, way, hop + 1).start())
                across(matrix, side, way, hop).start()

            when(hop <= far, pass_on)

    def gathered(matrix):
        for side in range(2):
            for way in range(2):
                for hop in range(1, reach(side, way) + 1):
                    across(matrix, side, way, hop, True).wait_recv()
        own_copies[matrix].wait()

    pair = me + 1 - 2 * odd
    onward, behind = me + 2 - 4 * odd, me - 2 + 4 * odd
    has_onward = (onward >= 0) & (onward < n)
    has_behind = (behind >= 0) & (behind < n)

    members = n // 2
    rank = lax.div(me, 2)

    def inside(device):
        return (device >= 2) & (device < n - 2)

    mid = inside(me)

    def rim(leg, block, received=False, keys_only=False):
        near, far = 2 * (1 - odd) * blocks + block, 2 * odd * blocks + block
        width_of = pl.ds(0, inner if keys_only else 2 * inner)
        if received:
            dst = kvs.at[far if leg else near, :, width_of]
        else:
            dst = kvs.at[far, :, width_of]
        src = kvs.at[near, :, width_of] if leg else kv.at[block]
        return remote(
            src, dst, rim_send.at[leg, block], rim_recv.at[leg, block],
            {"patch": onward if leg else pair},
        )

    def detour(leg, block, received=False):
        values = pl.ds(inner, inner)
        if leg:
            slot = (2 * odd if received else 2 * (1 - odd)) * blocks + block
            src, dst, target = transit.at[block], kvs.at[slot, :, values], pair
        else:
            src, dst, target = kv.at[block, :, values], transit.at[block], behind
        return remote(src, dst, side_send.at[leg, block], side_recv.at[leg, block], {"patch": target})

    def rim_start(block):
        rim(0, block).start()
        pl.when(has_behind & inside(behind))(lambda: detour(0, block).start())

    def rim_forward(block):
        rim(0, block, True).wait_recv()
        pl.when(has_onward & inside(onward))(lambda: rim(1, block, keys_only=True).start())
        pl.when(has_onward & jnp.logical_not(inside(onward)))(lambda: rim(1, block).start())

        @pl.when(mid)
        def _():
            detour(0, block, True).wait_recv()
            detour(1, block).start()

    def rim_arrive(block):
        pl.when(has_behind & jnp.logical_not(mid))(lambda: rim(1, block, True).wait_recv())

        @pl.when(mid)
        def _():
            rim(1, block, True, keys_only=True).wait_recv()
            detour(1, block, True).wait_recv()

    def rim_settle(block):
        rim(0, block).wait_send()
        pl.when(has_onward & inside(onward))(lambda: rim(1, block, keys_only=True).wait_send())
        pl.when(has_onward & jnp.logical_not(inside(onward)))(lambda: rim(1, block).wait_send())
        pl.when(has_behind & inside(behind))(lambda: detour(0, block).wait_send())
        pl.when(mid)(lambda: detour(1, block).wait_send())

    first_owner = members // 2 - 1
    low, quarter = lead // 2, lead // 4

    def project_text():
        fetch_text.wait()
        conditioned = (
            rows_in[...].astype(jnp.float32) * (1.0 + row_mod[1]) + row_mod[0]
        ).astype(jnp.bfloat16)

        @pl.loop(0, part.shape[1] // TILE)
        def _(index):
            window = pl.ds(pl.multiple_of(index * TILE, TILE), TILE)
            part[:, window] = jnp.dot(
                conditioned, out[pl.ds(0, wt.shape[0]), window], preferred_element_type=jnp.float32
            ).astype(part.dtype)

    def text_swap():
        return remote(
            part.at[span((1 - odd) * low, low)], fetched, text_send.at[0], text_recv.at[0], {"patch": pair}
        )

    def contribute(piece, received=None):
        owner = 2 * (first_owner + piece) + odd
        slot = rank if received is None else received
        return remote(
            folded.at[pl.ds(piece * quarter, quarter)], sums.at[slot],
            sums_send.at[piece], sums_recv.at[slot], {"patch": owner},
        )

    def share(piece, member):
        ref = text.at[span(odd * low + piece * quarter, quarter)]
        return remote(ref, ref, share_send.at[member], share_recv.at[piece], {"patch": 2 * member + odd})

    def text_back():
        ref = text.at[span(odd * low, low)]
        return remote(ref, ref, text_send.at[1], text_recv.at[1], {"patch": pair})

    def text_start():
        project_text()
        text_swap().start()
        pl.when(section == 0)(fetch_state.wait)

    def text_fold():
        text_swap().wait_recv()
        folded[...] = (
            part[span(odd * low, low), :].astype(jnp.float32) + fetched[...].astype(jnp.float32)
        ).astype(folded.dtype)
        for piece in range(2):
            pl.when(rank != first_owner + piece)(lambda: contribute(piece).start())

    def text_reduce():
        for piece in range(2):
            owner = first_owner + piece

            @pl.when(rank == owner)
            def _():
                added = folded[pl.ds(piece * quarter, quarter), :].astype(jnp.float32)
                for member in range(members):
                    if member != owner:
                        contribute(piece, member).wait_recv()
                        added = added + sums[member].astype(jnp.float32)
                total[...] = added.astype(total.dtype)
                keep = pltpu.make_async_copy(
                    total, text.at[span(odd * low + piece * quarter, quarter)], text_sem.at[0]
                )
                keep.start()
                keep.wait()
                for member in range(members):
                    if member != owner:
                        share(piece, member).start()

    def text_spread():
        for piece in range(2):
            pl.when(rank != first_owner + piece)(lambda: share(piece, 0).wait_recv())
        text_back().start()

    def text_arrive():
        own = text.at[span((1 - odd) * low, low)]
        remote(own, own, text_send.at[1], text_recv.at[1], {"patch": pair}).wait_recv()

    def text_settle():
        text_swap().wait_send()
        text_back().wait_send()
        for piece in range(2):
            owner = first_owner + piece
            pl.when(rank != owner)(lambda: contribute(piece).wait_send())

            @pl.when(rank == owner)
            def _():
                for member in range(members):
                    if member != owner:
                        share(piece, member).wait_send()

    def norm(source, first, last):
        @pl.loop(first, last)
        def _(index):
            window = pl.ds(pl.multiple_of(index * ROWS, ROWS), ROWS)
            values = source[window, :].astype(jnp.float32)
            center = values - jnp.mean(values, axis=-1, keepdims=True)
            variance = jnp.mean(center * center, axis=-1, keepdims=True)
            scaled = center * lax.rsqrt(variance + EPSILON)
            normed[window, :] = (
                scaled * (1.0 + modulation[1]) + modulation[0]
            ).astype(normed.dtype)

    def project_query(after):
        @pl.loop(0, inner // TILE)
        def _(index):
            window = pl.ds(pl.multiple_of(index * TILE, TILE), TILE)
            query[:, window] = jnp.dot(
                normed[...], wq_all[:, window], preferred_element_type=jnp.float32
            ).astype(query.dtype)
            after(index)

    together = 4 if heads % 4 == 0 else 1
    bunches = heads // together

    def attend(after):
        @pl.loop(0, blocks * bunches)
        def _(index):
            block = lax.div(index, bunches)
            bunch = lax.rem(index, bunches)
            rows = pl.ds(pl.multiple_of(block * BLK, BLK), BLK)
            limit = lead + counts[block] * BLK
            live = lax.broadcasted_iota(jnp.int32, (BLK, keys), 1) < limit
            picks = [
                jnp.clip(chosen[block, slot] - (me - 1) * blocks, 0, 3 * blocks - 1)
                for slot in range(spread)
            ]
            for one in range(together):
                start = bunch * (together * HD) + one * HD
                columns = pl.ds(pl.multiple_of(start, HD), HD)
                beyond = pl.ds(pl.multiple_of(inner + start, HD), HD)
                key = jnp.concatenate([text[:, columns]] + [kvs[pick, :, columns] for pick in picks], axis=0)
                value = jnp.concatenate([text[:, beyond]] + [kvs[pick, :, beyond] for pick in picks], axis=0)
                scores = lax.dot_general(
                    query[rows, columns], key, (((1,), (1,)), ((), ())),
                    preferred_element_type=jnp.float32,
                )
                scores = jnp.where(live, scores, -1e30)
                peak = jnp.max(scores, axis=-1, keepdims=True)
                raised = jnp.exp((scores - peak) * HD ** (-0.5))
                whole = jnp.sum(raised, axis=-1, keepdims=True)
                share_of = jnp.dot(
                    raised.astype(jnp.bfloat16), value, preferred_element_type=jnp.float32
                )
                mixed[rows, columns] = (share_of / whole).astype(mixed.dtype)
            after(index)

    parts = width // (3 * TILE) if width % (3 * TILE) == 0 else 1
    part_width = width // parts

    def project_out(source, index_from, index_to):
        @pl.loop(index_from, index_to)
        def _(index):
            window = pl.ds(pl.multiple_of(index * TILE, TILE), TILE)
            projected = jnp.dot(mixed[...], wo_all[:, window], preferred_element_type=jnp.float32)
            out[:, window] = (
                source[:, window].astype(jnp.float32) + modulation[2, :, window] * projected
            ).astype(out.dtype)

    def hand(index):
        window = pl.ds(index * part_width, part_width)
        return remote(
            out.at[:, window], inbox.at[:, window],
            hand_send.at[index], hand_recv.at[index], {"section": 1 - section},
        )

    def store(index):
        window = pl.ds(index * part_width, part_width)
        return pltpu.make_async_copy(out.at[:, window], final.at[:, window], final_sem.at[index])

    def wait_keys():
        own_copies[2].wait()
        for block in range(blocks):
            rim_arrive(block)
        text_arrive()

    steps = 2 * half
    tiles = tokens // ROWS

    def open_gate(index):
        pl.semaphore_signal(gate.at[index], inc=1, device_id={"section": 1 - section}, device_id_type=MESH)

    each = part_width // TILE
    calls = inner // TILE

    def relay_at(pairs):
        def after(index):
            for when_index, step in pairs:
                pl.when(index == when_index)(lambda: relay(1, step))
        return after

    strip = 2 * wo.shape[0]
    split = strip % HD == 0 and half > 1

    def gathered_near(last):
        for side in range(2):
            for way in range(2):
                far = reach(side, way)
                for hop in range(1, far + 1):
                    if (hop == half) == last:
                        across(1, side, way, hop, True).wait_recv()
        if not last:
            own_copies[1].wait()

    def project_near():
        far_strip = lax.div(at(place + half), 2)

        @pl.loop(0, width // TILE)
        def _(index):
            window = pl.ds(pl.multiple_of(index * TILE, TILE), TILE)
            partial = None
            for other in range(1, members):
                strip_at = pl.multiple_of(lax.rem(far_strip + other, members) * strip, HD)
                term = jnp.dot(
                    mixed[:, pl.ds(strip_at, strip)], wo_all[pl.ds(strip_at, strip), window],
                    preferred_element_type=jnp.float32,
                )
                partial = term if partial is None else partial + term
            gathering[:, window] = inbox[:, window].astype(jnp.float32) + modulation[2, :, window] * partial

    def project_far(index_from, index_to):
        strip_at = pl.multiple_of(lax.div(at(place + half), 2) * strip, HD)

        @pl.loop(index_from, index_to)
        def _(index):
            window = pl.ds(pl.multiple_of(index * TILE, TILE), TILE)
            term = jnp.dot(
                mixed[:, pl.ds(strip_at, strip)], wo_all[pl.ds(strip_at, strip), window],
                preferred_element_type=jnp.float32,
            )
            out[:, window] = (gathering[:, window] + modulation[2, :, window] * term).astype(out.dtype)

    edge = members == 4
    ring_size = n - 4
    ring_half = ring_size // 2
    spot = (1 - odd) * (rank - 1) + odd * (ring_size - rank)

    def inner_at(position):
        position = lax.rem(position + ring_size, ring_size)
        high = lax.div(position, ring_half)
        return 2 + (1 - high) * 2 * position + high * (2 * (ring_size - 1 - position) + 1)

    def partner_of(device):
        return device + 2 - 4 * lax.rem(lax.div(device, 2), 2)

    partner = partner_of(me)
    inner_rows = wq.shape[0]
    inner_apart = exclusive_rows(inner_rows, PHI)
    inner_keep = inner_rows - inner_apart
    inner_cut = wq.shape[1] // 2

    def inner_reach(kind, side, way):
        return ring_half - (kind + side + way) % 2

    def inner_piece(device, side, every=True):
        start = (device * inner_rows if every else 0) + parity * inner_apart
        return (wq_all if every else wq).at[span(start, inner_keep), pl.ds(side * inner_cut, inner_cut)]

    def inner_ring(kind, side, way, hop, received=False):
        home = inner_at(spot + ways[way] * (hop if received else hop - 1))
        dst = inner_piece(partner_of(home) if kind else home, side)
        src = inner_piece(me, side, False) if hop == 1 and not kind and not received else dst
        target = inner_at(spot - 1) if way else inner_at(spot + 1)
        flow = kind * 4 + side * 2 + way
        return remote(src, dst, inner_send.at[flow, hop - 1], inner_recv.at[flow, hop - 1], {"patch": target})

    def inner_across(kind, side, way, hop, received=False):
        home = inner_at(spot + ways[way] * hop)
        shard = partner_of(home) if kind else home
        whose = 1 - parity if received else parity
        ref = wq_all.at[
            span(shard * inner_rows + whose * inner_keep, inner_apart), pl.ds(side * inner_cut, inner_cut)
        ]
        flow = kind * 4 + side * 2 + way
        return remote(ref, ref, cross_send.at[flow, hop], cross_recv.at[flow, hop], {"groups": mate})

    def inject(side, received=False):
        dst = inner_piece(partner if received else me, side)
        return remote(
            inner_piece(me, side, False), dst, inject_send.at[side], inject_recv.at[side], {"patch": partner}
        )

    def inner_launch():
        @pl.when(mid)
        def _():
            for side in range(2):
                for way in range(2):
                    inner_ring(0, side, way, 1).start()

        @pl.when(jnp.logical_not(mid))
        def _():
            for side in range(2):
                inject(side).start()

    def inner_pass(kind, side, hop):
        for way in range(2):
            far = inner_reach(kind, side, way)
            if hop <= far:
                inner_ring(kind, side, way, hop, received=True).wait_recv()
                if hop < far:
                    inner_ring(kind, side, way, hop + 1).start()
                inner_across(kind, side, way, hop).start()

    def inner_relay(step):
        turn, side = step // 2, step % 2
        if turn > 3:
            return

        @pl.when(mid)
        def _():
            if turn == 0:
                inject(side, True).wait_recv()
                for way in range(2):
                    inner_ring(1, side, way, 1).start()
                inner_across(1, side, 0, 0).start()
            inner_pass(turn % 2, side, turn // 2 + 1)

    def inner_messages():
        for kind in range(2):
            for side in range(2):
                for way in range(2):
                    for hop in range(1, inner_reach(kind, side, way) + 1):
                        yield kind, side, way, hop

    def guest_part(index):
        share_of = tokens // GUESTS
        window = pl.ds(index * share_of, share_of)
        return remote(
            normed.at[window], guest.at[window], guest_send.at[index], guest_recv.at[index], {"patch": partner}
        )

    def give_back(index):
        window = pl.ds(index * TILE if isinstance(index, int) else pl.multiple_of(index * TILE, TILE), TILE)
        return remote(
            answer.at[:, window], query.at[:, window], back_send.at[index], back_recv.at[index], {"patch": partner}
        )

    def inner_norm(step):
        if step < GUESTS:
            norm(inbox, step * tiles // GUESTS, (step + 1) * tiles // GUESTS)
            pl.when(jnp.logical_not(mid))(lambda: guest_part(step).start())

    def inner_query(*pairs):
        own_copies[0].wait()

        @pl.when(mid)
        def _():
            for side in range(2):
                inner_across(1, side, 0, 0, True).wait_recv()
            for message in inner_messages():
                inner_across(*message, received=True).wait_recv()
            for index in range(GUESTS):
                guest_part(index).wait_recv()

            @pl.loop(0, calls)
            def _(index):
                window = pl.ds(pl.multiple_of(index * TILE, TILE), TILE)
                answer[:, window] = jnp.dot(
                    guest[...], wq_all[:, window], preferred_element_type=jnp.float32
                ).astype(answer.dtype)
                give_back(index).start()

            project_query(relay_at(pairs))

        @pl.when(jnp.logical_not(mid))
        def _():
            for _, step in pairs:
                relay(1, step)
            for index in range(calls):
                give_back(index).wait_recv()

    def inner_settle():
        @pl.when(mid)
        def _():
            for side in range(2):
                inner_across(1, side, 0, 0).wait_send()
            for message in inner_messages():
                inner_across(*message).wait_send()
                inner_ring(*message).wait_send()
            for index in range(calls):
                give_back(index).wait_send()

        @pl.when(jnp.logical_not(mid))
        def _():
            for side in range(2):
                inject(side).wait_send()
            for index in range(GUESTS):
                guest_part(index).wait_send()

    def finish(index):
        project_out(inbox, index * each, (index + 1) * each)

    actions = {
        "launch": launch,
        "copies": lambda: [copy.start() for copy in own_copies],
        "keys": rim_start,
        "forward": rim_forward,
        "text": text_start,
        "fold": text_fold,
        "reduce": text_reduce,
        "spread": text_spread,
        "norm": lambda index: norm(inbox, index * tiles // steps, (index + 1) * tiles // steps),
        "relay": relay,
        "open": open_gate,
        "pass": lambda index: pl.semaphore_wait(gate.at[index], 1),
        "query": lambda *pairs: (gathered(0), project_query(relay_at(pairs))),
        "attend": lambda *pairs: (wait_keys(), attend(relay_at(pairs))),
    }

    inner_actions = {
        "launch": lambda matrix: launch(1) if matrix else inner_launch(),
        "norm": inner_norm,
        "relay": lambda matrix, step: relay(1, step) if matrix else inner_relay(step),
        "query": inner_query,
    }

    def play(script, own={}):
        for name, *values in script:
            own.get(name, actions[name])(*values)

    @pl.when(section == 0)
    def _():
        fetch_text.start()
        fetch_state.start()
        play(script_first(steps, blocks), inner_actions if edge else {})
        gathered(1)
        for index in range(parts):
            finish(index)
            hand(index).start()
            store(index).start()

    @pl.when(section == 1)
    def _():
        fetch_text.start()
        early, late = script_second(steps, blocks)
        play(early)
        for index in range(parts):
            hand(index).wait_recv()
        norm(inbox, 0, tiles)
        play(late)
        if split:
            gathered_near(False)
            project_near()
            gathered_near(True)
        else:
            gathered(1)
        for index in range(parts):
            if split:
                project_far(index * each, (index + 1) * each)
            else:
                finish(index)
            store(index).start()

    def settle(matrix):
        for side in range(2):
            for way in range(2):
                for hop in range(1, reach(side, way) + 1):
                    across(matrix, side, way, hop).wait_send()
                    ring(matrix, side, way, hop).wait_send()

    if edge:
        pl.when(section == 0)(inner_settle)
        pl.when(section == 1)(lambda: settle(0))
    else:
        settle(0)
    settle(1)
    text_settle()
    for block in range(blocks):
        rim_settle(block)

    for index in range(parts):
        store(index).wait()

    @pl.when(section == 0)
    def _():
        for index in range(parts):
            hand(index).wait_send()


def run(n, chosen, counts, modulation, rows_in, row_mod, state, wq, wo, kv, wt):
    half = n // 2
    tokens, width = state.shape
    inner = wq.shape[1]
    lead = rows_in.shape[0]
    pairs = kv.shape[2]
    blocks = kv.shape[0]
    smem = pl.BlockSpec(memory_space=pltpu.SMEM)
    vmem = pl.BlockSpec(memory_space=pltpu.VMEM)
    anywhere = pl.BlockSpec(memory_space=pl.ANY)
    dma = pltpu.SemaphoreType.DMA
    parts = width // (3 * TILE) if width % (3 * TILE) == 0 else 1
    b16 = jnp.bfloat16
    return pl.pallas_call(
        functools.partial(kernel, n),
        out_shape=jax.ShapeDtypeStruct(state.shape, state.dtype),
        in_specs=[smem, smem] + [vmem] * 3 + [anywhere] * 5,
        out_specs=anywhere,
        scratch_shapes=[
            pltpu.VMEM((n * wq.shape[0], inner), b16),
            pltpu.VMEM((n * wo.shape[0], width), b16),
            pltpu.VMEM((3 * blocks,) + kv.shape[1:], b16),
            pltpu.VMEM((lead, pairs), b16),
            pltpu.VMEM((lead, pairs), b16),
            pltpu.VMEM((lead // 2, pairs), b16),
            pltpu.VMEM((lead // 2, pairs), b16),
            pltpu.VMEM((half, lead // 4, pairs), b16),
            pltpu.VMEM((lead // 4, pairs), b16),
            pltpu.VMEM((tokens, width), b16),
            pltpu.VMEM((tokens, inner), b16),
            pltpu.VMEM((tokens, inner), b16),
            pltpu.VMEM((tokens, width), b16),
            pltpu.VMEM((tokens, width), b16),
            pltpu.VMEM((tokens, width), jnp.float32),
            pltpu.VMEM((blocks, BLK, inner), b16),
            pltpu.VMEM((tokens, width), b16),
            pltpu.VMEM((tokens, inner), b16),
            dma((8, half)), dma((8, half)), dma((8, half)), dma((8, half)),
            dma((2, blocks)), dma((2, blocks)), dma((2, blocks)), dma((2, blocks)),
            dma((8, 2)), dma((8, 2)), dma((8, 3)), dma((8, 3)), dma((2,)), dma((2,)), dma((GUESTS,)), dma((GUESTS,)),
            dma((inner // TILE,)), dma((inner // TILE,)),
            dma((2,)), dma((2,)), dma((2,)), dma((half,)), dma((half,)), dma((2,)),
            dma((parts,)), dma((parts,)), dma((5,)), dma((1,)), dma((parts,)),
            pltpu.SemaphoreType.REGULAR((3,)),
        ],
        compiler_params=pltpu.CompilerParams(
            collective_id=0, has_side_effects=True, vmem_limit_bytes=60 * 2**20
        ),
        name="layers",
    )(chosen, counts, modulation, rows_in, row_mod, state, wq, wo, kv, wt)


def local(
    hidden_in, text_rows, mod_table, timestep, w_query, w_out, w_text, stale_kv, mask_blocks, counts
):
    patch_id = lax.axis_index("patch")
    n = lax.axis_size("patch")
    width = text_rows.shape[1]
    modulation = lax.dynamic_index_in_dim(mod_table, timestep[0], 0, keepdims=False)[0]
    modulation = modulation[:, None]
    row_mod = lax.dynamic_slice_in_dim(modulation[3:5], patch_id * width, width, 2)
    kv = stale_kv[0].reshape(-1, BLK, stale_kv.shape[2])
    result = run(
        n, mask_blocks, counts, modulation, text_rows, row_mod, hidden_in, w_query[0], w_out[0], kv, w_text[0]
    )
    return result[None]


def solution(mesh):
    in_specs = (
        P(("groups", "patch"), None),
        P("groups", "patch"),
        P(None, "section", None, None),
        P("groups"),
        P("section", "patch", None),
        P("section", "patch", None),
        P("section", "patch", None),
        P("section", ("groups", "patch"), None),
        P(("groups", "patch"), None),
        P(("groups", "patch")),
    )
    out_specs = P("section", ("groups", "patch"), None)
    return jax.shard_map(local, mesh=mesh, in_specs=in_specs, out_specs=out_specs, check_vma=False)
```

```python
import functools

import jax
import jax.numpy as jnp
from jax import lax
from jax.experimental import pallas as pl
from jax.experimental.pallas import tpu as pltpu
from jax.sharding import PartitionSpec as P

HD = 128
BLK = 128
EPSILON = 1e-06
MESH = pl.DeviceIdType.MESH
ROWS = 16


def exclusive_rows(rows, twelfths):
    return max(rows * twelfths // 12 // ROWS, 1) * ROWS


TILE = 256
GUESTS = 8
PHI = 5


def script_first(steps, blocks):
    sends, onward, text = (0, 2, 4), (2, 4, 6), (1, 3, 5)
    out = [("launch", 0)] + [("launch", 1)]
    out += [("keys", b) for b in range(blocks) if sends[b] < 0] + [("copies",), ("text",)]
    for s in range(steps):
        out += [("norm", s), ("relay", 0, s)]
        if 0 and s == 2: out += [("launch", 1)]
        if s >= 0: out += [("relay", 1, s - 0)]
        out += [("keys", b) for b in range(blocks) if sends[b] == s]
        if s == text[0]: out += [("fold",)]
        out += [("forward", b) for b in range(blocks) if onward[b] == s]
        if s == text[1]: out += [("reduce",)]
        if s == text[2]: out += [("spread",)]
        if s == 6: out += [("open", 0)]
    rest = list(range(steps - 0, steps))
    out += [("query",) + tuple(zip((5,), rest)), ("attend",) + tuple(zip((2, 5, 8), rest[1:]))]
    return out


def script_second(steps, blocks):
    sends, onward, text = (0, 2, 4), (2, 4, 6), (1, 3, 5)
    out = [("copies",), ("text",), ("pass", 0), ("launch", 0)]
    out += [("keys", b) for b in range(blocks) if sends[b] < 0]
    for s in range(steps):
        out += [("relay", 0, s)]
        if s == 2: out += [("launch", 1)]
        if s >= 4: out += [("relay", 1, s - 4)]
        out += [("keys", b) for b in range(blocks) if sends[b] == s]
        if s == text[0]: out += [("fold",)]
        out += [("forward", b) for b in range(blocks) if onward[b] == s]
        if s == text[1]: out += [("reduce",)]
        if s == text[2]: out += [("spread",)]
    rest = list(range(steps - 4, steps))
    return out, [("query",) + tuple(zip((5,), rest)), ("attend",) + tuple(zip((2, 5, 8), rest[1:]))]

def kernel(
    n, chosen, counts, modulation, rows_in, row_mod, state, wq, wo, kv, wt, final,
    wq_all, wo_all, kvs, text, part, fetched, folded, sums, total, normed, query, mixed, inbox, out, gathering, transit, guest, answer,
    ring_send, ring_recv, mate_send, mate_recv, rim_send, rim_recv, side_send, side_recv,
    inner_send, inner_recv, cross_send, cross_recv, inject_send, inject_recv, guest_send, guest_recv, back_send, back_recv,
    text_send, text_recv, sums_send, sums_recv, share_send, share_recv, hand_send, hand_recv, own_sem, text_sem, final_sem, gate,
):
    me = lax.axis_index("patch")
    group = lax.axis_index("groups")
    section = lax.axis_index("section")
    parity = lax.rem(group, 2)
    mate = group + 1 - 2 * parity
    half = n // 2
    odd = lax.rem(me, 2)
    place = (1 - odd) * lax.div(me, 2) + odd * (n - 1 - lax.div(me, 2))
    tokens, width = state.shape
    inner = query.shape[1]
    heads = inner // HD
    blocks = kv.shape[0]
    spread = chosen.shape[1]
    lead = text.shape[0]
    keys = lead + spread * BLK

    def at(position):
        position = lax.rem(position + n, n)
        high = lax.div(position, half)
        return (1 - high) * 2 * position + high * (2 * (n - 1 - position) + 1)

    def when(condition, action):
        if isinstance(condition, bool):
            if condition:
                action()
        else:
            pl.when(condition)(action)

    right, left = at(place + 1), at(place - 1)

    own_copies = [
        pltpu.make_async_copy(wq, wq_all.at[pl.ds(pl.multiple_of(me * wq.shape[0], ROWS), wq.shape[0])], own_sem.at[0]),
        pltpu.make_async_copy(wo, wo_all.at[pl.ds(pl.multiple_of(me * wo.shape[0], ROWS), wo.shape[0])], own_sem.at[1]),
        pltpu.make_async_copy(kv, kvs.at[pl.ds(blocks, blocks)], own_sem.at[2]),
    ]
    fetch_text = pltpu.make_async_copy(wt, out.at[pl.ds(0, wt.shape[0])], own_sem.at[3])
    fetch_state = pltpu.make_async_copy(state, inbox, own_sem.at[4])

    barrier = pltpu.get_barrier_semaphore()
    for step in range(1, n):
        pl.semaphore_signal(barrier, inc=1, device_id={"patch": lax.rem(me + step, n)}, device_id_type=MESH)
    pl.semaphore_signal(barrier, inc=1, device_id={"groups": mate}, device_id_type=MESH)
    pl.semaphore_signal(barrier, inc=1, device_id={"section": 1 - section}, device_id_type=MESH)
    pl.semaphore_wait(barrier, n + 1)

    matrices = ((wq, wq_all), (wo, wo_all))
    ways = (-1, 1)

    def reach(side, way):
        return half - (side + way) % 2

    def remote(src, dst, send, recv, target):
        return pltpu.make_async_remote_copy(
            src_ref=src, dst_ref=dst, send_sem=send, recv_sem=recv,
            device_id=target, device_id_type=MESH,
        )

    def span(start, size, unit=ROWS):
        return pl.ds(start if isinstance(start, int) else pl.multiple_of(start, unit), size)

    def ring(matrix, side, way, hop, received=False, first=False):
        own, every = matrices[matrix]
        rows, cut = own.shape[0], own.shape[1] // 2
        apart = exclusive_rows(rows, 5 if matrix else 6)
        keep = rows - apart
        columns = span(side * cut, cut, HD)
        shard = at(place + ways[way] * (hop if received else hop - 1))
        dst = every.at[span(shard * rows + parity * apart, keep), columns]
        src = own.at[span(parity * apart, keep), columns] if first else dst
        target = {"patch": left if way else right}
        flow = matrix * 4 + side * 2 + way
        return remote(src, dst, ring_send.at[flow, hop - 1], ring_recv.at[flow, hop - 1], target)

    def across(matrix, side, way, hop, received=False):
        own, every = matrices[matrix]
        rows, cut = own.shape[0], own.shape[1] // 2
        apart = exclusive_rows(rows, 5 if matrix else 6)
        keep = rows - apart
        shard = at(place + ways[way] * hop)
        whose = 1 - parity if received else parity
        ref = every.at[span(shard * rows + whose * keep, apart), span(side * cut, cut, HD)]
        flow = matrix * 4 + side * 2 + way
        return remote(ref, ref, mate_send.at[flow, hop - 1], mate_recv.at[flow, hop - 1], {"groups": mate})

    def launch(matrix):
        for side in range(2):
            for way in range(2):
                ring(matrix, side, way, 1, first=True).start()

    def relay(matrix, step):
        hop, side = step // 2 + 1, step % 2
        for way in range(2):
            far = reach(side, way)

            def pass_on():
                ring(matrix, side, way, hop, received=True).wait_recv()
                when(hop < far, lambda: ring(matrix, side, way, hop + 1).start())
                across(matrix, side, way, hop).start()

            when(hop <= far, pass_on)

    def gathered(matrix):
        for side in range(2):
            for way in range(2):
                for hop in range(1, reach(side, way) + 1):
                    across(matrix, side, way, hop, True).wait_recv()
        own_copies[matrix].wait()

    pair = me + 1 - 2 * odd
    onward, behind = me + 2 - 4 * odd, me - 2 + 4 * odd
    has_onward = (onward >= 0) & (onward < n)
    has_behind = (behind >= 0) & (behind < n)

    members = n // 2
    rank = lax.div(me, 2)

    def inside(device):
        return (device >= 2) & (device < n - 2)

    mid = inside(me)

    def rim(leg, block, received=False, keys_only=False):
        near, far = 2 * (1 - odd) * blocks + block, 2 * odd * blocks + block
        width_of = pl.ds(0, inner if keys_only else 2 * inner)
        if received:
            dst = kvs.at[far if leg else near, :, width_of]
        else:
            dst = kvs.at[far, :, width_of]
        src = kvs.at[near, :, width_of] if leg else kv.at[block]
        return remote(
            src, dst, rim_send.at[leg, block], rim_recv.at[leg, block],
            {"patch": onward if leg else pair},
        )

    def detour(leg, block, received=False):
        values = pl.ds(inner, inner)
        if leg:
            slot = (2 * odd if received else 2 * (1 - odd)) * blocks + block
            src, dst, target = transit.at[block], kvs.at[slot, :, values], pair
        else:
            src, dst, target = kv.at[block, :, values], transit.at[block], behind
        return remote(src, dst, side_send.at[leg, block], side_recv.at[leg, block], {"patch": target})

    def rim_start(block):
        rim(0, block).start()
        pl.when(has_behind & inside(behind))(lambda: detour(0, block).start())

    def rim_forward(block):
        rim(0, block, True).wait_recv()
        pl.when(has_onward & inside(onward))(lambda: rim(1, block, keys_only=True).start())
        pl.when(has_onward & jnp.logical_not(inside(onward)))(lambda: rim(1, block).start())

        @pl.when(mid)
        def _():
            detour(0, block, True).wait_recv()
            detour(1, block).start()

    def rim_arrive(block):
        pl.when(has_behind & jnp.logical_not(mid))(lambda: rim(1, block, True).wait_recv())

        @pl.when(mid)
        def _():
            rim(1, block, True, keys_only=True).wait_recv()
            detour(1, block, True).wait_recv()

    def rim_settle(block):
        rim(0, block).wait_send()
        pl.when(has_onward & inside(onward))(lambda: rim(1, block, keys_only=True).wait_send())
        pl.when(has_onward & jnp.logical_not(inside(onward)))(lambda: rim(1, block).wait_send())
        pl.when(has_behind & inside(behind))(lambda: detour(0, block).wait_send())
        pl.when(mid)(lambda: detour(1, block).wait_send())

    first_owner = members // 2 - 1
    low, quarter = lead // 2, lead // 4

    def project_text():
        fetch_text.wait()
        conditioned = (
            rows_in[...].astype(jnp.float32) * (1.0 + row_mod[1]) + row_mod[0]
        ).astype(jnp.bfloat16)

        @pl.loop(0, part.shape[1] // TILE)
        def _(index):
            window = pl.ds(pl.multiple_of(index * TILE, TILE), TILE)
            part[:, window] = jnp.dot(
                conditioned, out[pl.ds(0, wt.shape[0]), window], preferred_element_type=jnp.float32
            ).astype(part.dtype)

    def text_swap():
        return remote(
            part.at[span((1 - odd) * low, low)], fetched, text_send.at[0], text_recv.at[0], {"patch": pair}
        )

    def contribute(piece, received=None):
        owner = 2 * (first_owner + piece) + odd
        slot = rank if received is None else received
        return remote(
            folded.at[pl.ds(piece * quarter, quarter)], sums.at[slot],
            sums_send.at[piece], sums_recv.at[slot], {"patch": owner},
        )

    def share(piece, member):
        ref = text.at[span(odd * low + piece * quarter, quarter)]
        return remote(ref, ref, share_send.at[member], share_recv.at[piece], {"patch": 2 * member + odd})

    def text_back():
        ref = text.at[span(odd * low, low)]
        return remote(ref, ref, text_send.at[1], text_recv.at[1], {"patch": pair})

    def text_start():
        project_text()
        text_swap().start()
        pl.when(section == 0)(fetch_state.wait)

    def text_fold():
        text_swap().wait_recv()
        folded[...] = (
            part[span(odd * low, low), :].astype(jnp.float32) + fetched[...].astype(jnp.float32)
        ).astype(folded.dtype)
        for piece in range(2):
            pl.when(rank != first_owner + piece)(lambda: contribute(piece).start())

    def text_reduce():
        for piece in range(2):
            owner = first_owner + piece

            @pl.when(rank == owner)
            def _():
                added = folded[pl.ds(piece * quarter, quarter), :].astype(jnp.float32)
                for member in range(members):
                    if member != owner:
                        contribute(piece, member).wait_recv()
                        added = added + sums[member].astype(jnp.float32)
                total[...] = added.astype(total.dtype)
                keep = pltpu.make_async_copy(
                    total, text.at[span(odd * low + piece * quarter, quarter)], text_sem.at[0]
                )
                keep.start()
                keep.wait()
                for member in range(members):
                    if member != owner:
                        share(piece, member).start()

    def text_spread():
        for piece in range(2):
            pl.when(rank != first_owner + piece)(lambda: share(piece, 0).wait_recv())
        text_back().start()

    def text_arrive():
        own = text.at[span((1 - odd) * low, low)]
        remote(own, own, text_send.at[1], text_recv.at[1], {"patch": pair}).wait_recv()

    def text_settle():
        text_swap().wait_send()
        text_back().wait_send()
        for piece in range(2):
            owner = first_owner + piece
            pl.when(rank != owner)(lambda: contribute(piece).wait_send())

            @pl.when(rank == owner)
            def _():
                for member in range(members):
                    if member != owner:
                        share(piece, member).wait_send()

    def norm(source, first, last):
        @pl.loop(first, last)
        def _(index):
            window = pl.ds(pl.multiple_of(index * ROWS, ROWS), ROWS)
            values = source[window, :].astype(jnp.float32)
            center = values - jnp.mean(values, axis=-1, keepdims=True)
            variance = jnp.mean(center * center, axis=-1, keepdims=True)
            scaled = center * lax.rsqrt(variance + EPSILON)
            normed[window, :] = (
                scaled * (1.0 + modulation[1]) + modulation[0]
            ).astype(normed.dtype)

    def project_query(after):
        @pl.loop(0, inner // TILE)
        def _(index):
            window = pl.ds(pl.multiple_of(index * TILE, TILE), TILE)
            query[:, window] = jnp.dot(
                normed[...], wq_all[:, window], preferred_element_type=jnp.float32
            ).astype(query.dtype)
            after(index)

    together = 4 if heads % 4 == 0 else 1
    bunches = heads // together

    def attend(after):
        @pl.loop(0, blocks * bunches)
        def _(index):
            block = lax.div(index, bunches)
            bunch = lax.rem(index, bunches)
            rows = pl.ds(pl.multiple_of(block * BLK, BLK), BLK)
            limit = lead + counts[block] * BLK
            live = lax.broadcasted_iota(jnp.int32, (BLK, keys), 1) < limit
            picks = [
                jnp.clip(chosen[block, slot] - (me - 1) * blocks, 0, 3 * blocks - 1)
                for slot in range(spread)
            ]
            for one in range(together):
                start = bunch * (together * HD) + one * HD
                columns = pl.ds(pl.multiple_of(start, HD), HD)
                beyond = pl.ds(pl.multiple_of(inner + start, HD), HD)
                key = jnp.concatenate([text[:, columns]] + [kvs[pick, :, columns] for pick in picks], axis=0)
                value = jnp.concatenate([text[:, beyond]] + [kvs[pick, :, beyond] for pick in picks], axis=0)
                scores = lax.dot_general(
                    query[rows, columns], key, (((1,), (1,)), ((), ())),
                    preferred_element_type=jnp.float32,
                )
                scores = jnp.where(live, scores, -1e30)
                peak = jnp.max(scores, axis=-1, keepdims=True)
                raised = jnp.exp((scores - peak) * HD ** (-0.5))
                whole = jnp.sum(raised, axis=-1, keepdims=True)
                share_of = jnp.dot(
                    raised.astype(jnp.bfloat16), value, preferred_element_type=jnp.float32
                )
                mixed[rows, columns] = (share_of / whole).astype(mixed.dtype)
            after(index)

    parts = width // (3 * TILE) if width % (3 * TILE) == 0 else 1
    part_width = width // parts

    def project_out(source, index_from, index_to):
        @pl.loop(index_from, index_to)
        def _(index):
            window = pl.ds(pl.multiple_of(index * TILE, TILE), TILE)
            projected = jnp.dot(mixed[...], wo_all[:, window], preferred_element_type=jnp.float32)
            out[:, window] = (
                source[:, window].astype(jnp.float32) + modulation[2, :, window] * projected
            ).astype(out.dtype)

    def hand(index):
        window = pl.ds(index * part_width, part_width)
        return remote(
            out.at[:, window], inbox.at[:, window],
            hand_send.at[index], hand_recv.at[index], {"section": 1 - section},
        )

    def store(index):
        window = pl.ds(index * part_width, part_width)
        return pltpu.make_async_copy(out.at[:, window], final.at[:, window], final_sem.at[index])

    def wait_keys():
        own_copies[2].wait()
        for block in range(blocks):
            rim_arrive(block)
        text_arrive()

    steps = 2 * half
    tiles = tokens // ROWS

    def open_gate(index):
        pl.semaphore_signal(gate.at[index], inc=1, device_id={"section": 1 - section}, device_id_type=MESH)

    each = part_width // TILE
    calls = inner // TILE

    def relay_at(pairs):
        def after(index):
            for when_index, step in pairs:
                pl.when(index == when_index)(lambda: relay(1, step))
        return after

    strip = 2 * wo.shape[0]
    split = strip % HD == 0 and half > 1

    def gathered_near(last):
        for side in range(2):
            for way in range(2):
                far = reach(side, way)
                for hop in range(1, far + 1):
                    if (hop == half) == last:
                        across(1, side, way, hop, True).wait_recv()
        if not last:
            own_copies[1].wait()

    def project_near():
        far_strip = lax.div(at(place + half), 2)

        @pl.loop(0, width // TILE)
        def _(index):
            window = pl.ds(pl.multiple_of(index * TILE, TILE), TILE)
            partial = None
            for other in range(1, members):
                strip_at = pl.multiple_of(lax.rem(far_strip + other, members) * strip, HD)
                term = jnp.dot(
                    mixed[:, pl.ds(strip_at, strip)], wo_all[pl.ds(strip_at, strip), window],
                    preferred_element_type=jnp.float32,
                )
                partial = term if partial is None else partial + term
            gathering[:, window] = inbox[:, window].astype(jnp.float32) + modulation[2, :, window] * partial

    def project_far(index_from, index_to):
        strip_at = pl.multiple_of(lax.div(at(place + half), 2) * strip, HD)

        @pl.loop(index_from, index_to)
        def _(index):
            window = pl.ds(pl.multiple_of(index * TILE, TILE), TILE)
            term = jnp.dot(
                mixed[:, pl.ds(strip_at, strip)], wo_all[pl.ds(strip_at, strip), window],
                preferred_element_type=jnp.float32,
            )
            out[:, window] = (gathering[:, window] + modulation[2, :, window] * term).astype(out.dtype)

    edge = members == 4
    ring_size = n - 4
    ring_half = ring_size // 2
    spot = (1 - odd) * (rank - 1) + odd * (ring_size - rank)

    def inner_at(position):
        position = lax.rem(position + ring_size, ring_size)
        high = lax.div(position, ring_half)
        return 2 + (1 - high) * 2 * position + high * (2 * (ring_size - 1 - position) + 1)

    def partner_of(device):
        return device + 2 - 4 * lax.rem(lax.div(device, 2), 2)

    partner = partner_of(me)
    inner_rows = wq.shape[0]
    inner_apart = exclusive_rows(inner_rows, PHI)
    inner_keep = inner_rows - inner_apart
    inner_cut = wq.shape[1] // 2

    def inner_reach(kind, side, way):
        return ring_half - (kind + side + way) % 2

    def inner_piece(device, side, every=True):
        start = (device * inner_rows if every else 0) + parity * inner_apart
        return (wq_all if every else wq).at[span(start, inner_keep), pl.ds(side * inner_cut, inner_cut)]

    def inner_ring(kind, side, way, hop, received=False):
        home = inner_at(spot + ways[way] * (hop if received else hop - 1))
        dst = inner_piece(partner_of(home) if kind else home, side)
        src = inner_piece(me, side, False) if hop == 1 and not kind and not received else dst
        target = inner_at(spot - 1) if way else inner_at(spot + 1)
        flow = kind * 4 + side * 2 + way
        return remote(src, dst, inner_send.at[flow, hop - 1], inner_recv.at[flow, hop - 1], {"patch": target})

    def inner_across(kind, side, way, hop, received=False):
        home = inner_at(spot + ways[way] * hop)
        shard = partner_of(home) if kind else home
        whose = 1 - parity if received else parity
        ref = wq_all.at[
            span(shard * inner_rows + whose * inner_keep, inner_apart), pl.ds(side * inner_cut, inner_cut)
        ]
        flow = kind * 4 + side * 2 + way
        return remote(ref, ref, cross_send.at[flow, hop], cross_recv.at[flow, hop], {"groups": mate})

    def inject(side, received=False):
        dst = inner_piece(partner if received else me, side)
        return remote(
            inner_piece(me, side, False), dst, inject_send.at[side], inject_recv.at[side], {"patch": partner}
        )

    def inner_launch():
        @pl.when(mid)
        def _():
            for side in range(2):
                for way in range(2):
                    inner_ring(0, side, way, 1).start()

        @pl.when(jnp.logical_not(mid))
        def _():
            for side in range(2):
                inject(side).start()

    def inner_pass(kind, side, hop):
        for way in range(2):
            far = inner_reach(kind, side, way)
            if hop <= far:
                inner_ring(kind, side, way, hop, received=True).wait_recv()
                if hop < far:
                    inner_ring(kind, side, way, hop + 1).start()
                inner_across(kind, side, way, hop).start()

    def inner_relay(step):
        turn, side = step // 2, step % 2
        if turn > 3:
            return

        @pl.when(mid)
        def _():
            if turn == 0:
                inject(side, True).wait_recv()
                for way in range(2):
                    inner_ring(1, side, way, 1).start()
                inner_across(1, side, 0, 0).start()
            inner_pass(turn % 2, side, turn // 2 + 1)

    def inner_messages():
        for kind in range(2):
            for side in range(2):
                for way in range(2):
                    for hop in range(1, inner_reach(kind, side, way) + 1):
                        yield kind, side, way, hop

    def guest_part(index):
        share_of = tokens // GUESTS
        window = pl.ds(index * share_of, share_of)
        return remote(
            normed.at[window], guest.at[window], guest_send.at[index], guest_recv.at[index], {"patch": partner}
        )

    def give_back(index):
        window = pl.ds(index * TILE if isinstance(index, int) else pl.multiple_of(index * TILE, TILE), TILE)
        return remote(
            answer.at[:, window], query.at[:, window], back_send.at[index], back_recv.at[index], {"patch": partner}
        )

    def inner_norm(step):
        if step < GUESTS:
            norm(inbox, step * tiles // GUESTS, (step + 1) * tiles // GUESTS)
            pl.when(jnp.logical_not(mid))(lambda: guest_part(step).start())

    def inner_query(*pairs):
        own_copies[0].wait()

        @pl.when(mid)
        def _():
            for side in range(2):
                inner_across(1, side, 0, 0, True).wait_recv()
            for message in inner_messages():
                inner_across(*message, received=True).wait_recv()
            for index in range(GUESTS):
                guest_part(index).wait_recv()

            @pl.loop(0, calls)
            def _(index):
                window = pl.ds(pl.multiple_of(index * TILE, TILE), TILE)
                answer[:, window] = jnp.dot(
                    guest[...], wq_all[:, window], preferred_element_type=jnp.float32
                ).astype(answer.dtype)
                give_back(index).start()

            project_query(relay_at(pairs))

        @pl.when(jnp.logical_not(mid))
        def _():
            for _, step in pairs:
                relay(1, step)
            for index in range(calls):
                give_back(index).wait_recv()

    def inner_settle():
        @pl.when(mid)
        def _():
            for side in range(2):
                inner_across(1, side, 0, 0).wait_send()
            for message in inner_messages():
                inner_across(*message).wait_send()
                inner_ring(*message).wait_send()
            for index in range(calls):
                give_back(index).wait_send()

        @pl.when(jnp.logical_not(mid))
        def _():
            for side in range(2):
                inject(side).wait_send()
            for index in range(GUESTS):
                guest_part(index).wait_send()

    def finish(index):
        project_out(inbox, index * each, (index + 1) * each)

    actions = {
        "launch": launch,
        "copies": lambda: [copy.start() for copy in own_copies],
        "keys": rim_start,
        "forward": rim_forward,
        "text": text_start,
        "fold": text_fold,
        "reduce": text_reduce,
        "spread": text_spread,
        "norm": lambda index: norm(inbox, index * tiles // steps, (index + 1) * tiles // steps),
        "relay": relay,
        "open": open_gate,
        "pass": lambda index: pl.semaphore_wait(gate.at[index], 1),
        "query": lambda *pairs: (gathered(0), project_query(relay_at(pairs))),
        "attend": lambda *pairs: (wait_keys(), attend(relay_at(pairs))),
    }

    inner_actions = {
        "launch": lambda matrix: launch(1) if matrix else inner_launch(),
        "norm": inner_norm,
        "relay": lambda matrix, step: relay(1, step) if matrix else inner_relay(step),
        "query": inner_query,
    }

    def play(script, own={}):
        for name, *values in script:
            own.get(name, actions[name])(*values)

    @pl.when(section == 0)
    def _():
        fetch_text.start()
        fetch_state.start()
        play(script_first(steps, blocks), inner_actions if edge else {})
        gathered(1)
        for index in range(parts):
            finish(index)
            hand(index).start()
            store(index).start()

    @pl.when(section == 1)
    def _():
        fetch_text.start()
        early, late = script_second(steps, blocks)
        play(early)
        for index in range(parts):
            hand(index).wait_recv()
        norm(inbox, 0, tiles)
        play(late)
        if split:
            gathered_near(False)
            project_near()
            gathered_near(True)
        else:
            gathered(1)
        for index in range(parts):
            if split:
                project_far(index * each, (index + 1) * each)
            else:
                finish(index)
            store(index).start()

    def settle(matrix):
        for side in range(2):
            for way in range(2):
                for hop in range(1, reach(side, way) + 1):
                    across(matrix, side, way, hop).wait_send()
                    ring(matrix, side, way, hop).wait_send()

    if edge:
        pl.when(section == 0)(inner_settle)
        pl.when(section == 1)(lambda: settle(0))
    else:
        settle(0)
    settle(1)
    text_settle()
    for block in range(blocks):
        rim_settle(block)

    for index in range(parts):
        store(index).wait()

    @pl.when(section == 0)
    def _():
        for index in range(parts):
            hand(index).wait_send()


def run(n, chosen, counts, modulation, rows_in, row_mod, state, wq, wo, kv, wt):
    half = n // 2
    tokens, width = state.shape
    inner = wq.shape[1]
    lead = rows_in.shape[0]
    pairs = kv.shape[2]
    blocks = kv.shape[0]
    smem = pl.BlockSpec(memory_space=pltpu.SMEM)
    vmem = pl.BlockSpec(memory_space=pltpu.VMEM)
    anywhere = pl.BlockSpec(memory_space=pl.ANY)
    dma = pltpu.SemaphoreType.DMA
    parts = width // (3 * TILE) if width % (3 * TILE) == 0 else 1
    b16 = jnp.bfloat16
    return pl.pallas_call(
        functools.partial(kernel, n),
        out_shape=jax.ShapeDtypeStruct(state.shape, state.dtype),
        in_specs=[smem, smem] + [vmem] * 3 + [anywhere] * 5,
        out_specs=anywhere,
        scratch_shapes=[
            pltpu.VMEM((n * wq.shape[0], inner), b16),
            pltpu.VMEM((n * wo.shape[0], width), b16),
            pltpu.VMEM((3 * blocks,) + kv.shape[1:], b16),
            pltpu.VMEM((lead, pairs), b16),
            pltpu.VMEM((lead, pairs), b16),
            pltpu.VMEM((lead // 2, pairs), b16),
            pltpu.VMEM((lead // 2, pairs), b16),
            pltpu.VMEM((half, lead // 4, pairs), b16),
            pltpu.VMEM((lead // 4, pairs), b16),
            pltpu.VMEM((tokens, width), b16),
            pltpu.VMEM((tokens, inner), b16),
            pltpu.VMEM((tokens, inner), b16),
            pltpu.VMEM((tokens, width), b16),
            pltpu.VMEM((tokens, width), b16),
            pltpu.VMEM((tokens, width), jnp.float32),
            pltpu.VMEM((blocks, BLK, inner), b16),
            pltpu.VMEM((tokens, width), b16),
            pltpu.VMEM((tokens, inner), b16),
            dma((8, half)), dma((8, half)), dma((8, half)), dma((8, half)),
            dma((2, blocks)), dma((2, blocks)), dma((2, blocks)), dma((2, blocks)),
            dma((8, 2)), dma((8, 2)), dma((8, 3)), dma((8, 3)), dma((2,)), dma((2,)), dma((GUESTS,)), dma((GUESTS,)),
            dma((inner // TILE,)), dma((inner // TILE,)),
            dma((2,)), dma((2,)), dma((2,)), dma((half,)), dma((half,)), dma((2,)),
            dma((parts,)), dma((parts,)), dma((5,)), dma((1,)), dma((parts,)),
            pltpu.SemaphoreType.REGULAR((3,)),
        ],
        compiler_params=pltpu.CompilerParams(
            collective_id=0, has_side_effects=True, vmem_limit_bytes=60 * 2**20
        ),
        name="layers",
    )(chosen, counts, modulation, rows_in, row_mod, state, wq, wo, kv, wt)


def local(
    hidden_in, text_rows, mod_table, timestep, w_query, w_out, w_text, stale_kv, mask_blocks, counts
):
    patch_id = lax.axis_index("patch")
    n = lax.axis_size("patch")
    width = text_rows.shape[1]
    modulation = lax.dynamic_index_in_dim(mod_table, timestep[0], 0, keepdims=False)[0]
    modulation = modulation[:, None]
    row_mod = lax.dynamic_slice_in_dim(modulation[3:5], patch_id * width, width, 2)
    kv = stale_kv[0].reshape(-1, BLK, stale_kv.shape[2])
    result = run(
        n, mask_blocks, counts, modulation, text_rows, row_mod, hidden_in, w_query[0], w_out[0], kv, w_text[0]
    )
    return result[None]


def solution(mesh):
    in_specs = (
        P(("groups", "patch"), None),
        P("groups", "patch"),
        P(None, "section", None, None),
        P("groups"),
        P("section", "patch", None),
        P("section", "patch", None),
        P("section", "patch", None),
        P("section", ("groups", "patch"), None),
        P(("groups", "patch"), None),
        P(("groups", "patch")),
    )
    out_specs = P("section", ("groups", "patch"), None)
    return jax.shard_map(local, mesh=mesh, in_specs=in_specs, out_specs=out_specs, check_vma=False)
```
